32 devices in a mesh: seq: 8 (over z, x), tensor: 4 (over y, core).
Axes of the slice: x: 2, y: 2, z: 4, core: 2. Of those that a mesh axis runs over, the one named last changes fastest.
Arguments:
- latents: bfloat16 [1024, 2560], P('seq'), may hold values from -6 to 6
- levels: int32 [8], P('seq'), may hold values from 0 to 999
- head_slot: int32 [1], replicated, may hold values from 0 to 7
- fresh_noise: bfloat16 [128, 2560], P(None, 'tensor'), may hold values from -6 to 6
- ada_weight: bfloat16 [256, 3, 2560], P(None, None, 'tensor'), may hold values from -0.375 to 0.375
- qkv_weight: bfloat16 [2560, 3, 1536], P(None, None, 'tensor'), may hold values from -0.125 to 0.125
- q_gain: float32 [128], replicated, may hold values from 0.5 to 2.5
- k_gain: float32 [128], replicated, may hold values from 0.5 to 2.5
- out_weight: bfloat16 [1536, 2560], P('tensor'), may hold values from -0.15625 to 0.15625
Outputs:
- window: bfloat16 [1024, 2560], P('seq', 'tensor')
- clean: bfloat16 [128, 2560], P('seq', 'tensor')
The draws below stay inside these ranges and needn't reach their ends.
All inputs are finite; a program needn't handle non-finite values.
Results may differ from the reference program's by a relative error of at most 0.0053.
Values may be sent and summed in bfloat16 or wider, within the bound.
A program may use at most 64 MiB of HBM per device.

```python
import math
import jax
import jax.numpy as jnp
from jax import lax

D = 2560
HEADS = 12
HD = 128
TEMB = 256
LEVELS = 1000
GROUP = 128
GROUPS = 8
FRAMES = 1024


def set_ends(drawn, rng, least, high):
    dims = drawn.shape
    place = [jax.random.randint(jax.random.fold_in(rng, axis), (), 0, dims[axis]) for axis in range(len(dims))]
    drawn = drawn.at[tuple(place)].set(least)
    longest = dims.index(max(dims))
    place[longest] = (place[longest] + 1) % dims[longest]
    return drawn.at[tuple(place)].set(high)


def block_levels(key, dims, cuts, least, top_value):
    loudness, own = 1.0, jax.random.fold_in(key, 6)
    for position, shards_of in cuts:
        draws = jnp.exp(jax.random.uniform(jax.random.fold_in(own, position), (shards_of,), jnp.float32, least / len(cuts), top_value / len(cuts)))
        loudness = loudness * jnp.repeat(draws, dims[position] // shards_of).reshape([-1 if axis == position else 1 for axis in range(len(dims))])
    return loudness


def noise(key, shape, scale, limit, cuts=(), held_as=jnp.bfloat16):
    factor_of = block_levels(key, shape, cuts, -0.22, 0.18) if cuts else 1.0
    array = jax.random.normal(key, shape, jnp.float32) * scale * factor_of
    return jnp.minimum(jnp.maximum(array, -limit), limit).astype(held_as)


def setup_inputs(seed: int = 0) -> dict:
    splits = jax.random.split(jax.random.key(seed), 10)
    return {
        "latents": noise(splits[0], (FRAMES, D), 1.0, 6.0, ((0, 8),)),
        "levels": set_ends(jax.random.randint(splits[1], (GROUPS,), 0, LEVELS), jax.random.fold_in(splits[1], 1), 0, LEVELS - 1).astype(jnp.int32),
        "head_slot": jax.random.randint(splits[2], (1,), 0, GROUPS).astype(jnp.int32),
        "fresh_noise": noise(splits[3], (GROUP, D), 1.0, 6.0, ((1, 4),)),
        "ada_weight": noise(splits[4], (TEMB, 3, D), TEMB ** -0.5, 0.375, ((2, 4),)),
        "qkv_weight": noise(splits[5], (D, 3, HEADS * HD), D ** -0.5, 0.125, ((2, 4),)),
        "q_gain": jnp.clip(jnp.exp(jax.random.uniform(splits[6], (HD,), jnp.float32, math.log(0.5), math.log(2.5))), 0.5, 2.5),
        "k_gain": jnp.clip(jnp.exp(jax.random.uniform(splits[7], (HD,), jnp.float32, math.log(0.5), math.log(2.5))), 0.5, 2.5),
        "out_weight": noise(splits[8], (HEADS * HD, D), (HEADS * HD) ** -0.5, 0.15625, ((0, 4),)),
    }


def modulation(levels, ada_weight):
    half_width = TEMB // 2
    frequency = jnp.exp(-math.log(10000.0) * jnp.arange(half_width, dtype=jnp.float32) / half_width)
    angles = levels.astype(jnp.float32)[:, None] * frequency[None, :]
    embedding = jax.nn.silu(jnp.concatenate([jnp.cos(angles), jnp.sin(angles)], axis=1)).astype(jnp.bfloat16)
    flat = jnp.dot(embedding, ada_weight.reshape(TEMB, 3 * D), preferred_element_type=jnp.float32)
    return flat.reshape(-1, 3, D)

def modulate(states, offset_terms, scale_terms):
    average = lax.optimization_barrier(jnp.mean(states, axis=-1, keepdims=True))
    centered = states - average
    variance = lax.optimization_barrier(jnp.mean(centered * centered, axis=-1, keepdims=True))
    normed = centered * lax.rsqrt(variance + 1e-06)
    return (normed * (1.0 + scale_terms) + offset_terms).astype(jnp.bfloat16)

def rms_scaled(matrix, gain_vector, factor):
    power = lax.optimization_barrier(jnp.mean(matrix * matrix, axis=-1, keepdims=True))
    return (matrix * lax.rsqrt(power + 1e-06) * gain_vector * factor).astype(jnp.bfloat16)

def project(hidden, qkv_weight, q_gain, k_gain):
    projected_all = jnp.dot(hidden, qkv_weight.reshape(D, 3 * HEADS * HD), preferred_element_type=jnp.float32)
    projected_all = projected_all.reshape(-1, 3, HEADS, HD)
    queries = rms_scaled(projected_all[:, 0], q_gain, 1.0 / math.sqrt(HD))
    keys = rms_scaled(projected_all[:, 1], k_gain, 1.0)
    values = projected_all[:, 2].astype(jnp.bfloat16)
    return (queries, keys, values)

def reference(latents, levels, head_slot, fresh_noise, ada_weight, qkv_weight, q_gain, k_gain, out_weight):
    oldest = head_slot[0].astype(jnp.int32)
    modulations = modulation(levels, ada_weight)
    states = latents.astype(jnp.float32).reshape(GROUPS, GROUP, D)
    hidden = modulate(states, modulations[:, 0][:, None], modulations[:, 1][:, None]).reshape(GROUPS * GROUP, D)
    queries, keys, values = project(hidden, qkv_weight, q_gain, k_gain)
    query_blocks = queries.reshape(GROUPS, GROUP, HEADS, HD)
    key_blocks = keys.reshape(GROUPS, GROUP, HEADS, HD)
    value_blocks = values.reshape(GROUPS, GROUP, HEADS, HD)
    block_ranks = (jnp.arange(GROUPS, dtype=jnp.int32) - oldest) % GROUPS

    def one_block(query_index):
        query_tile = query_blocks[query_index].astype(jnp.float32)
        initial = (jnp.zeros((HEADS, GROUP), jnp.float32), jnp.zeros((GROUP, HEADS, HD), jnp.float32))

        def absorb(state_now, key_index):

            def update_state(state_old):
                running_sum, weighted = state_old
                key_tile = key_blocks[key_index].astype(jnp.float32)
                value_tile = value_blocks[key_index].astype(jnp.float32)
                scores = jnp.einsum('qhd,khd->hqk', query_tile, key_tile)
                weights = jnp.exp(scores)
                running_sum = running_sum + lax.optimization_barrier(jnp.sum(weights, axis=-1))
                rounded = lax.optimization_barrier(weights.astype(jnp.bfloat16)).astype(jnp.float32)
                weighted = weighted + jnp.einsum('hqk,khd->qhd', rounded, value_tile)
                return (running_sum, weighted)

            def keep_state(state_old):
                return state_old
            visible = block_ranks[key_index] <= block_ranks[query_index]
            return (lax.cond(visible, update_state, keep_state, state_now), None)
        finished, unused = lax.scan(absorb, initial, jnp.arange(GROUPS, dtype=jnp.int32))
        return (finished[1] / finished[0].T[..., None]).astype(jnp.bfloat16)
    attended = lax.map(one_block, jnp.arange(GROUPS, dtype=jnp.int32)).reshape(GROUPS * GROUP, HEADS * HD)
    projected = jnp.dot(attended, out_weight, preferred_element_type=jnp.float32).reshape(GROUPS, GROUP, D)
    updated = (states + modulations[:, 2][:, None] * projected).astype(jnp.bfloat16)
    clean = lax.dynamic_index_in_dim(updated, oldest, 0, keepdims=False)
    leaving = (block_ranks == 0)[:, None, None]
    window = jnp.where(leaving, fresh_noise[None], updated).reshape(GROUPS * GROUP, D)
    return (window, clean)
```

```python
import functools
import math

import jax
import jax.numpy as jnp
from jax import lax
from jax.experimental import pallas as pl
from jax.experimental.pallas import tpu as pltpu
from jax.sharding import PartitionSpec as P

F32 = jnp.float32
BF16 = jnp.bfloat16
EPS = 1e-06


def embed(levels, width):
    half_width = width // 2
    frequency = jnp.exp(-math.log(10000.0) * jnp.arange(half_width, dtype=F32) / half_width)
    angles = levels.astype(F32)[:, None] * frequency[None, :]
    return jax.nn.silu(jnp.concatenate([jnp.cos(angles), jnp.sin(angles)], axis=1)).astype(BF16)


def dot(a, b):
    return jnp.dot(a, b, preferred_element_type=F32)


def dot_t(a, b):
    return lax.dot_general(a, b, (((1,), (1,)), ((), ())), preferred_element_type=F32)


def kernel(
    n, parts, slab, clean_rows,
    head_ref, emb_ref, gains_ref, lat_hbm, noise_ref, ada_hbm, qkv_hbm, out_hbm,
    window_ref, clean_ref,
    lat, ada, wqkv, wout, normed, hidden, mods, gates, lat_rows, kv, queries, q_rows,
    acc, totals, attended, sums_out, sums_in, own_sum,
    load_sem, mod_send, mod_recv, gate_send, gate_recv, row_send, row_recv,
    kv_send, kv_recv, q_send, q_recv, sum_send, sum_recv,
):
    me = lax.axis_index("seq")
    part = lax.axis_index("tensor")
    rows, width = lat.shape
    columns = window_ref.shape[1]
    head_size = gains_ref.shape[1]
    heads = queries.shape[1] // head_size

    def remote(src, dst, send, recv, axis, target):
        return pltpu.make_async_remote_copy(
            src_ref=src, dst_ref=dst, send_sem=send, recv_sem=recv,
            device_id={axis: target}, device_id_type=pl.DeviceIdType.MESH,
        )

    loads = [
        pltpu.make_async_copy(ada_hbm, ada, load_sem.at[0]),
        pltpu.make_async_copy(lat_hbm, lat, load_sem.at[1]),
        pltpu.make_async_copy(qkv_hbm.at[1], wqkv.at[1], load_sem.at[2]),
        pltpu.make_async_copy(qkv_hbm.at[2], wqkv.at[2], load_sem.at[3]),
        pltpu.make_async_copy(qkv_hbm.at[0], wqkv.at[0], load_sem.at[4]),
        pltpu.make_async_copy(out_hbm, wout, load_sem.at[5]),
    ]
    for load in loads:
        load.start()

    barrier = pltpu.get_barrier_semaphore()
    for step in range(1, parts):
        pl.semaphore_signal(
            barrier, inc=1, device_id={"tensor": lax.rem(part + step, parts)},
            device_id_type=pl.DeviceIdType.MESH,
        )

    @pl.loop(1, n)
    def _(step):
        pl.semaphore_signal(
            barrier, inc=1, device_id={"seq": lax.rem(me + step, n)},
            device_id_type=pl.DeviceIdType.MESH,
        )

    loads[0].wait()
    emb = jnp.broadcast_to(emb_ref[...], (16, emb_ref.shape[1]))
    terms = [dot(emb, ada[j])[0:1] for j in range(3)]
    mine = jnp.concatenate(terms + [jnp.zeros((5, columns), F32)], axis=0)
    mods[part] = mine
    gates[me] = mine

    pl.semaphore_wait(barrier, n - 1 + parts - 1)

    def mod_copy(slot, target):
        return remote(
            mods.at[slot], mods.at[slot], mod_send.at[target], mod_recv.at[slot], "tensor", target
        )

    for step in range(1, parts):
        mod_copy(part, lax.rem(part + step, parts)).start()

    loads[1].wait()

    def slab_of(device):
        return pl.multiple_of((device * clean_rows) // slab * slab, slab)

    first_column = pl.multiple_of(part * columns, 128)

    def gate_copy(slot, target):
        return remote(
            gates.at[slot], gates.at[slot], gate_send.at[target], gate_recv.at[slot], "seq", target
        )

    def row_copy(slot, target):
        return remote(
            lat.at[pl.ds(slab_of(target), slab), pl.ds(first_column, columns)],
            lat_rows.at[slot], row_send.at[target], row_recv.at[slot], "seq", target,
        )

    own_slab = slab_of(me)
    lat_rows[me] = lat[pl.ds(own_slab, slab), pl.ds(first_column, columns)]

    tile = 16

    @pl.loop(0, rows // tile)
    def _(index):
        at = pl.ds(pl.multiple_of(index * tile, tile), tile)
        states = lat[at, :].astype(F32)
        centered = states - jnp.mean(states, axis=-1, keepdims=True)
        variance = jnp.mean(centered * centered, axis=-1, keepdims=True)
        normed[at, :] = centered * lax.rsqrt(variance + EPS)

    for step in range(1, parts):
        mod_copy(lax.rem(part + step, parts), part).wait_recv()
    for index in range(parts):
        at = slice(index * columns, (index + 1) * columns)
        hidden[:, at] = (
            normed[:, at] * (1.0 + mods[index, 1:2, :]) + mods[index, 0:1, :]
        ).astype(BF16)

    def scaled(matrix, gain, factor):
        power = jnp.mean(matrix * matrix, axis=-1, keepdims=True)
        return (matrix * lax.rsqrt(power + EPS) * gain * factor).astype(BF16)

    def kv_copy(kind, slot, target):
        return remote(
            kv.at[slot, kind], kv.at[slot, kind],
            kv_send.at[kind, target], kv_recv.at[kind, slot], "seq", target,
        )

    def q_copy(slot, target):
        return remote(
            queries.at[pl.ds(slab_of(target), slab), :], q_rows.at[slot],
            q_send.at[target], q_recv.at[slot], "seq", target,
        )

    def head_at(index):
        return slice(index * head_size, (index + 1) * head_size)

    loads[2].wait()
    raw = dot(hidden[...], wqkv[1])
    for h in range(heads):
        kv[me, 0, :, head_at(h)] = scaled(raw[:, head_at(h)], gains_ref[1:2, :], 1.0)

    @pl.loop(1, n)
    def _(step):
        kv_copy(0, me, lax.rem(me + step, n)).start()

    loads[3].wait()
    kv[me, 1] = dot(hidden[...], wqkv[2]).astype(BF16)

    @pl.loop(1, n)
    def _(step):
        kv_copy(1, me, lax.rem(me + step, n)).start()

    loads[4].wait()
    raw = dot(hidden[...], wqkv[0])
    for h in range(heads):
        queries[:, head_at(h)] = scaled(
            raw[:, head_at(h)], gains_ref[0:1, :], 1.0 / math.sqrt(head_size)
        )
    q_rows[me] = queries[pl.ds(own_slab, slab), :]

    @pl.loop(1, n)
    def _(step):
        target = lax.rem(me + step, n)
        q_copy(me, target).start()
        gate_copy(me, target).start()
        row_copy(me, target).start()

    oldest = head_ref[0]
    own_rank = lax.rem(me - oldest + n, n)

    for h in range(heads):
        weights = jnp.exp(dot_t(queries[:, head_at(h)], kv[me, 0, :, head_at(h)]))
        totals[:, head_at(h)] = weights
        acc[:, head_at(h)] = dot(weights.astype(BF16), kv[me, 1, :, head_at(h)])

    @pl.loop(1, n)
    def _(step):
        source = lax.rem(me - step + n, n)
        kv_copy(0, source, me).wait_recv()
        kv_copy(1, source, me).wait_recv()
        rank = lax.rem(source - oldest + n, n)
        seen = jnp.full((rows, rows), rank, jnp.int32) <= own_rank
        for h in range(heads):
            scores = dot_t(queries[:, head_at(h)], kv[source, 0, :, head_at(h)])
            weights = jnp.where(seen, jnp.exp(scores), 0.0)
            totals[:, head_at(h)] += weights
            acc[:, head_at(h)] += dot(weights.astype(BF16), kv[source, 1, :, head_at(h)])

    @pl.loop(1, n)
    def _(step):
        source = lax.rem(me - step + n, n)
        q_copy(source, me).wait_recv()
        gate_copy(source, me).wait_recv()
        row_copy(source, me).wait_recv()

    for h in range(heads):
        total = jnp.sum(totals[:, head_at(h)], axis=-1, keepdims=True)
        attended[0:rows, head_at(h)] = (acc[:, head_at(h)] / total).astype(BF16)
        weights = jnp.exp(dot_t(q_rows[oldest, :, head_at(h)], kv[oldest, 0, :, head_at(h)]))
        total = jnp.sum(weights, axis=-1, keepdims=True)
        product = dot(weights.astype(BF16), kv[oldest, 1, :, head_at(h)])
        attended[rows:, head_at(h)] = (product / total).astype(BF16)

    def sum_copy(slot, target):
        return remote(
            sums_out.at[target], sums_in.at[slot], sum_send.at[target], sum_recv.at[slot],
            "tensor", target,
        )

    loads[5].wait()
    for step in range(1, parts):
        target = lax.rem(part + step, parts)
        at = pl.ds(pl.multiple_of(target * columns, 128), columns)
        sums_out[target] = dot(attended[...], wout[:, at]).astype(BF16)
        sum_copy(part, target).start()
    own_sum[...] = dot(attended[...], wout[:, pl.ds(first_column, columns)])
    for step in range(1, parts):
        sum_copy(lax.rem(part + step, parts), part).wait_recv()

    total = own_sum[...]
    for step in range(1, parts):
        total += sums_in[lax.rem(part + step, parts)].astype(F32)
    own_states = lat[:, pl.ds(first_column, columns)].astype(F32)
    updated = (own_states + gates[me, 2:3, :] * total[0:rows]).astype(BF16)
    leaving = jnp.full((rows, columns), own_rank, jnp.int32) == 0
    window_ref[...] = jnp.where(leaving, noise_ref[...], updated)
    clean_ref[...] = (
        lat_rows[oldest].astype(F32) + gates[oldest, 2:3, :] * total[rows:]
    ).astype(BF16)

    for step in range(1, parts):
        target = lax.rem(part + step, parts)
        mod_copy(part, target).wait_send()
        sum_copy(part, target).wait_send()

    @pl.loop(1, n)
    def _(step):
        target = lax.rem(me + step, n)
        kv_copy(0, me, target).wait_send()
        kv_copy(1, me, target).wait_send()
        q_copy(me, target).wait_send()
        gate_copy(me, target).wait_send()
        row_copy(me, target).wait_send()


def local(
    latents, levels, head_slot, fresh_noise, ada_weight, qkv_weight, q_gain, k_gain, out_weight
):
    n = lax.axis_size("seq")
    parts = lax.axis_size("tensor")
    rows, width = latents.shape
    columns = fresh_noise.shape[1]
    inner = out_weight.shape[0]
    clean_rows = rows // n
    slab = max(clean_rows, 16)
    embedding = embed(levels, ada_weight.shape[0])
    gains = jnp.stack([q_gain, k_gain])
    vmem = pl.BlockSpec(memory_space=pltpu.VMEM)
    hbm = pl.BlockSpec(memory_space=pl.ANY)
    dma = pltpu.SemaphoreType.DMA
    window, clean = pl.pallas_call(
        functools.partial(kernel, n, parts, slab, clean_rows),
        out_shape=(
            jax.ShapeDtypeStruct((rows, columns), BF16),
            jax.ShapeDtypeStruct((slab, columns), BF16),
        ),
        in_specs=[
            pl.BlockSpec(memory_space=pltpu.SMEM), vmem, vmem, hbm, vmem, hbm, hbm, hbm,
        ],
        out_specs=(vmem, vmem),
        scratch_shapes=[
            pltpu.VMEM((rows, width), BF16),
            pltpu.VMEM((3, ada_weight.shape[0], columns), BF16),
            pltpu.VMEM((3, width, inner), BF16),
            pltpu.VMEM((inner, width), BF16),
            pltpu.VMEM((rows, width), F32),
            pltpu.VMEM((rows, width), BF16),
            pltpu.VMEM((parts, 8, columns), F32),
            pltpu.VMEM((n, 8, columns), F32),
            pltpu.VMEM((n, slab, columns), BF16),
            pltpu.VMEM((n, 2, rows, inner), BF16),
            pltpu.VMEM((rows, inner), BF16),
            pltpu.VMEM((n, slab, inner), BF16),
            pltpu.VMEM((rows, inner), F32),
            pltpu.VMEM((rows, inner), F32),
            pltpu.VMEM((rows + slab, inner), BF16),
            pltpu.VMEM((parts, rows + slab, columns), BF16),
            pltpu.VMEM((parts, rows + slab, columns), BF16),
            pltpu.VMEM((rows + slab, columns), F32),
            dma((6,)), dma((parts,)), dma((parts,)), dma((n,)), dma((n,)), dma((n,)), dma((n,)),
            dma((2, n)), dma((2, n)), dma((n,)), dma((n,)), dma((parts,)), dma((parts,)),
        ],
        compiler_params=pltpu.CompilerParams(
            collective_id=0, has_side_effects=True, vmem_limit_bytes=60 * 1024 * 1024
        ),
    )(
        head_slot, embedding, gains, latents, fresh_noise,
        jnp.transpose(ada_weight, (1, 0, 2)), jnp.transpose(qkv_weight, (1, 0, 2)), out_weight,
    )
    if clean_rows < slab:
        start = (lax.axis_index("seq") * clean_rows) % slab
        clean = lax.dynamic_slice_in_dim(clean, start, clean_rows, 0)
    return window, clean


def solution(mesh):
    return jax.shard_map(
        local,
        mesh=mesh,
        in_specs=(
            P("seq", None),
            P("seq"),
            P(),
            P(None, "tensor"),
            P(None, None, "tensor"),
            P(None, None, "tensor"),
            P(),
            P(),
            P("tensor", None),
        ),
        out_specs=(P("seq", "tensor"), P("seq", "tensor")),
        check_vma=False,
    )
```

```python
import functools
import math

import jax
import jax.numpy as jnp
from jax import lax
from jax.experimental import pallas as pl
from jax.experimental.pallas import tpu as pltpu
from jax.sharding import PartitionSpec as P

F32 = jnp.float32
BF16 = jnp.bfloat16
EPS = 1e-06


def embed(levels, width):
    half_width = width // 2
    frequency = jnp.exp(-math.log(10000.0) * jnp.arange(half_width, dtype=F32) / half_width)
    angles = levels.astype(F32)[:, None] * frequency[None, :]
    return jax.nn.silu(jnp.concatenate([jnp.cos(angles), jnp.sin(angles)], axis=1)).astype(BF16)


def dot(a, b):
    return jnp.dot(a, b, preferred_element_type=F32)


def dot_t(a, b):
    return lax.dot_general(a, b, (((1,), (1,)), ((), ())), preferred_element_type=F32)


def kernel(
    n, parts, slab, clean_rows,
    head_ref, emb_ref, gains_ref, lat_hbm, noise_ref, ada_hbm, qkv_hbm, out_hbm,
    window_ref, clean_ref,
    lat, ada, wqkv, wout, normed, hidden, mods, gates, lat_rows, kv, queries, q_rows,
    acc, totals, attended, sums_out, sums_in, own_sum,
    load_sem, mod_send, mod_recv, gate_send, gate_recv, row_send, row_recv,
    kv_send, kv_recv, q_send, q_recv, sum_send, sum_recv,
):
    me = lax.axis_index("seq")
    part = lax.axis_index("tensor")
    pair = 2
    side = lax.rem(me, pair)
    rows, width = lat.shape
    columns = window_ref.shape[1]
    head_size = gains_ref.shape[1]
    heads = queries.shape[1] // head_size

    def remote(src, dst, send, recv, axis, target):
        return pltpu.make_async_remote_copy(
            src_ref=src, dst_ref=dst, send_sem=send, recv_sem=recv,
            device_id={axis: target}, device_id_type=pl.DeviceIdType.MESH,
        )

    loads = [
        pltpu.make_async_copy(ada_hbm, ada, load_sem.at[0]),
        pltpu.make_async_copy(lat_hbm, lat, load_sem.at[1]),
        pltpu.make_async_copy(qkv_hbm.at[1], wqkv.at[1], load_sem.at[2]),
        pltpu.make_async_copy(qkv_hbm.at[2], wqkv.at[2], load_sem.at[3]),
        pltpu.make_async_copy(qkv_hbm.at[0], wqkv.at[0], load_sem.at[4]),
        pltpu.make_async_copy(out_hbm, wout, load_sem.at[5]),
    ]
    for load in loads:
        load.start()

    barrier = pltpu.get_barrier_semaphore()
    for step in range(1, parts):
        pl.semaphore_signal(
            barrier, inc=1, device_id={"tensor": lax.rem(part + step, parts)},
            device_id_type=pl.DeviceIdType.MESH,
        )

    @pl.loop(1, n)
    def _(step):
        pl.semaphore_signal(
            barrier, inc=1, device_id={"seq": lax.rem(me + step, n)},
            device_id_type=pl.DeviceIdType.MESH,
        )

    loads[0].wait()
    emb = jnp.broadcast_to(emb_ref[...], (16, emb_ref.shape[1]))
    terms = [dot(emb, ada[j])[0:1] for j in range(3)]
    mine = jnp.concatenate(terms + [jnp.zeros((5, columns), F32)], axis=0)
    mods[part] = mine
    gates[me] = mine

    pl.semaphore_wait(barrier, n - 1 + parts - 1)

    def mod_copy(slot, target):
        return remote(
            mods.at[slot], mods.at[slot], mod_send.at[target], mod_recv.at[slot], "tensor", target
        )

    for step in range(1, parts):
        mod_copy(part, lax.rem(part + step, parts)).start()

    loads[1].wait()

    def slab_of(device):
        return pl.multiple_of((device * clean_rows) // slab * slab, slab)

    first_column = pl.multiple_of(part * columns, 128)

    def gate_copy(slot, target):
        return remote(
            gates.at[slot], gates.at[slot], gate_send.at[target], gate_recv.at[slot], "seq", target
        )

    def row_copy(slot, target):
        return remote(
            lat.at[pl.ds(slab_of(target), slab), pl.ds(first_column, columns)],
            lat_rows.at[slot], row_send.at[target], row_recv.at[slot], "seq", target,
        )

    own_slab = slab_of(me)
    lat_rows[me] = lat[pl.ds(own_slab, slab), pl.ds(first_column, columns)]

    tile = 16

    @pl.loop(0, rows // tile)
    def _(index):
        at = pl.ds(pl.multiple_of(index * tile, tile), tile)
        states = lat[at, :].astype(F32)
        centered = states - jnp.mean(states, axis=-1, keepdims=True)
        variance = jnp.mean(centered * centered, axis=-1, keepdims=True)
        normed[at, :] = centered * lax.rsqrt(variance + EPS)

    for step in range(1, parts):
        mod_copy(lax.rem(part + step, parts), part).wait_recv()
    for index in range(parts):
        at = slice(index * columns, (index + 1) * columns)
        hidden[:, at] = (
            normed[:, at] * (1.0 + mods[index, 1:2, :]) + mods[index, 0:1, :]
        ).astype(BF16)

    def scaled(matrix, gain, factor):
        power = jnp.mean(matrix * matrix, axis=-1, keepdims=True)
        return (matrix * lax.rsqrt(power + EPS) * gain * factor).astype(BF16)

    def kv_copy(kind, slot, way, target):
        return remote(
            kv.at[slot, kind], kv.at[slot, kind],
            kv_send.at[kind, way, slot], kv_recv.at[kind, slot], "seq", target,
        )

    def onward(kind, slot, way, act):
        target = (me - pair, me + pair, me + 1 - 2 * side)[way]
        there = (target >= 0, target < n, None)[way]
        run = functools.partial(act, kind, slot, way, target)
        if there is None:
            run()
        else:
            pl.when(there)(run)

    def start(kind, slot, way, target):
        kv_copy(kind, slot, way, target).start()

    def finish(kind, slot, way, target):
        kv_copy(kind, slot, way, target).wait_send()

    def spread_out(kind, slot):
        for way in range(3):
            onward(kind, slot, way, start)

    def q_copy(slot, target):
        return remote(
            queries.at[pl.ds(slab_of(target), slab), :], q_rows.at[slot],
            q_send.at[target], q_recv.at[slot], "seq", target,
        )

    def head_at(index):
        return slice(index * head_size, (index + 1) * head_size)

    loads[2].wait()
    raw = dot(hidden[...], wqkv[1])
    for h in range(heads):
        kv[me, 0, :, head_at(h)] = scaled(raw[:, head_at(h)], gains_ref[1:2, :], 1.0)

    spread_out(0, me)

    loads[3].wait()
    kv[me, 1] = dot(hidden[...], wqkv[2]).astype(BF16)

    spread_out(1, me)

    loads[4].wait()
    raw = dot(hidden[...], wqkv[0])
    for h in range(heads):
        queries[:, head_at(h)] = scaled(
            raw[:, head_at(h)], gains_ref[0:1, :], 1.0 / math.sqrt(head_size)
        )
    q_rows[me] = queries[pl.ds(own_slab, slab), :]

    @pl.loop(1, n)
    def _(step):
        target = lax.rem(me + step, n)
        q_copy(me, target).start()
        gate_copy(me, target).start()
        row_copy(me, target).start()

    oldest = head_ref[0]
    own_rank = lax.rem(me - oldest + n, n)

    for h in range(heads):
        weights = jnp.exp(dot_t(queries[:, head_at(h)], kv[me, 0, :, head_at(h)]))
        totals[:, head_at(h)] = weights
        acc[:, head_at(h)] = dot(weights.astype(BF16), kv[me, 1, :, head_at(h)])

    def absorb(source):
        rank = lax.rem(source - oldest + n, n)
        seen = jnp.full((rows, rows), rank, jnp.int32) <= own_rank
        for h in range(heads):
            scores = dot_t(queries[:, head_at(h)], kv[source, 0, :, head_at(h)])
            weights = jnp.where(seen, jnp.exp(scores), 0.0)
            totals[:, head_at(h)] += weights
            acc[:, head_at(h)] += dot(weights.astype(BF16), kv[source, 1, :, head_at(h)])

    def take_across(source):
        kv_copy(0, source, 2, me).wait_recv()
        kv_copy(1, source, 2, me).wait_recv()
        absorb(source)

    other = me + 1 - 2 * side

    @pl.loop(1, n // pair)
    def _(step):
        below, above = me - step * pair, me + step * pair
        for kind in range(2):

            @pl.when(below >= 0)
            def _():
                kv_copy(kind, below, 1, me).wait_recv()
                onward(kind, below, 1, start)
                onward(kind, below, 2, start)

            @pl.when(above < n)
            def _():
                kv_copy(kind, above, 0, me).wait_recv()
                onward(kind, above, 0, start)
                onward(kind, above, 2, start)

        @pl.when(step == 1)
        def _():
            take_across(other)

        @pl.when((step > 1) & (other - (step - 1) * pair >= 0))
        def _():
            take_across(other - (step - 1) * pair)

        @pl.when((step > 1) & (other + (step - 1) * pair < n))
        def _():
            take_across(other + (step - 1) * pair)

        @pl.when(below >= 0)
        def _():
            absorb(below)

        @pl.when(above < n)
        def _():
            absorb(above)

    last = n - pair

    @pl.when(other - last >= 0)
    def _():
        take_across(other - last)

    @pl.when(other + last < n)
    def _():
        take_across(other + last)

    @pl.loop(1, n)
    def _(step):
        source = lax.rem(me - step + n, n)
        q_copy(source, me).wait_recv()
        gate_copy(source, me).wait_recv()
        row_copy(source, me).wait_recv()

    for h in range(heads):
        total = jnp.sum(totals[:, head_at(h)], axis=-1, keepdims=True)
        attended[0:rows, head_at(h)] = (acc[:, head_at(h)] / total).astype(BF16)
        weights = jnp.exp(dot_t(q_rows[oldest, :, head_at(h)], kv[oldest, 0, :, head_at(h)]))
        total = jnp.sum(weights, axis=-1, keepdims=True)
        product = dot(weights.astype(BF16), kv[oldest, 1, :, head_at(h)])
        attended[rows:, head_at(h)] = (product / total).astype(BF16)

    def sum_copy(slot, target):
        return remote(
            sums_out.at[target], sums_in.at[slot], sum_send.at[target], sum_recv.at[slot],
            "tensor", target,
        )

    loads[5].wait()
    for step in range(1, parts):
        target = lax.rem(part + step, parts)
        at = pl.ds(pl.multiple_of(target * columns, 128), columns)
        sums_out[target] = dot(attended[...], wout[:, at]).astype(BF16)
        sum_copy(part, target).start()
    own_sum[...] = dot(attended[...], wout[:, pl.ds(first_column, columns)])
    for step in range(1, parts):
        sum_copy(lax.rem(part + step, parts), part).wait_recv()

    total = own_sum[...]
    for step in range(1, parts):
        total += sums_in[lax.rem(part + step, parts)].astype(F32)
    own_states = lat[:, pl.ds(first_column, columns)].astype(F32)
    updated = (own_states + gates[me, 2:3, :] * total[0:rows]).astype(BF16)
    leaving = jnp.full((rows, columns), own_rank, jnp.int32) == 0
    window_ref[...] = jnp.where(leaving, noise_ref[...], updated)
    clean_ref[...] = (
        lat_rows[oldest].astype(F32) + gates[oldest, 2:3, :] * total[rows:]
    ).astype(BF16)

    for step in range(1, parts):
        target = lax.rem(part + step, parts)
        mod_copy(part, target).wait_send()
        sum_copy(part, target).wait_send()

    @pl.loop(1, n)
    def _(step):
        target = lax.rem(me + step, n)
        q_copy(me, target).wait_send()
        gate_copy(me, target).wait_send()
        row_copy(me, target).wait_send()

    for kind in range(2):
        for way in range(3):
            onward(kind, me, way, finish)

    @pl.loop(1, n // pair)
    def _(step):
        below, above = me - step * pair, me + step * pair
        for kind in range(2):

            @pl.when(below >= 0)
            def _():
                onward(kind, below, 1, finish)
                onward(kind, below, 2, finish)

            @pl.when(above < n)
            def _():
                onward(kind, above, 0, finish)
                onward(kind, above, 2, finish)


def local(
    latents, levels, head_slot, fresh_noise, ada_weight, qkv_weight, q_gain, k_gain, out_weight
):
    n = lax.axis_size("seq")
    parts = lax.axis_size("tensor")
    rows, width = latents.shape
    columns = fresh_noise.shape[1]
    inner = out_weight.shape[0]
    clean_rows = rows // n
    slab = max(clean_rows, 16)
    embedding = embed(levels, ada_weight.shape[0])
    gains = jnp.stack([q_gain, k_gain])
    vmem = pl.BlockSpec(memory_space=pltpu.VMEM)
    hbm = pl.BlockSpec(memory_space=pl.ANY)
    dma = pltpu.SemaphoreType.DMA
    window, clean = pl.pallas_call(
        functools.partial(kernel, n, parts, slab, clean_rows),
        out_shape=(
            jax.ShapeDtypeStruct((rows, columns), BF16),
            jax.ShapeDtypeStruct((slab, columns), BF16),
        ),
        in_specs=[
            pl.BlockSpec(memory_space=pltpu.SMEM), vmem, vmem, hbm, vmem, hbm, hbm, hbm,
        ],
        out_specs=(vmem, vmem),
        scratch_shapes=[
            pltpu.VMEM((rows, width), BF16),
            pltpu.VMEM((3, ada_weight.shape[0], columns), BF16),
            pltpu.VMEM((3, width, inner), BF16),
            pltpu.VMEM((inner, width), BF16),
            pltpu.VMEM((rows, width), F32),
            pltpu.VMEM((rows, width), BF16),
            pltpu.VMEM((parts, 8, columns), F32),
            pltpu.VMEM((n, 8, columns), F32),
            pltpu.VMEM((n, slab, columns), BF16),
            pltpu.VMEM((n, 2, rows, inner), BF16),
            pltpu.VMEM((rows, inner), BF16),
            pltpu.VMEM((n, slab, inner), BF16),
            pltpu.VMEM((rows, inner), F32),
            pltpu.VMEM((rows, inner), F32),
            pltpu.VMEM((rows + slab, inner), BF16),
            pltpu.VMEM((parts, rows + slab, columns), BF16),
            pltpu.VMEM((parts, rows + slab, columns), BF16),
            pltpu.VMEM((rows + slab, columns), F32),
            dma((6,)), dma((parts,)), dma((parts,)), dma((n,)), dma((n,)), dma((n,)), dma((n,)),
            dma((2, 3, n)), dma((2, n)), dma((n,)), dma((n,)), dma((parts,)), dma((parts,)),
        ],
        compiler_params=pltpu.CompilerParams(
            collective_id=0, has_side_effects=True, vmem_limit_bytes=60 * 1024 * 1024
        ),
    )(
        head_slot, embedding, gains, latents, fresh_noise,
        jnp.transpose(ada_weight, (1, 0, 2)), jnp.transpose(qkv_weight, (1, 0, 2)), out_weight,
    )
    if clean_rows < slab:
        start = (lax.axis_index("seq") * clean_rows) % slab
        clean = lax.dynamic_slice_in_dim(clean, start, clean_rows, 0)
    return window, clean


def solution(mesh):
    return jax.shard_map(
        local,
        mesh=mesh,
        in_specs=(
            P("seq", None),
            P("seq"),
            P(),
            P(None, "tensor"),
            P(None, None, "tensor"),
            P(None, None, "tensor"),
            P(),
            P(),
            P("tensor", None),
        ),
        out_specs=(P("seq", "tensor"), P("seq", "tensor")),
        check_vma=False,
    )
```

```python
import functools
import math

import jax
import jax.numpy as jnp
from jax import lax
from jax.experimental import pallas as pl
from jax.experimental.pallas import tpu as pltpu
from jax.sharding import PartitionSpec as P

F32 = jnp.float32
BF16 = jnp.bfloat16
EPS = 1e-06


def dot(a, b):
    return jnp.dot(a, b, preferred_element_type=F32)


def dot_t(a, b):
    return lax.dot_general(a, b, (((1,), (1,)), ((), ())), preferred_element_type=F32)


def kernel(
    n, parts, slab, clean_rows,
    head_ref, level_ref, q_gain_ref, k_gain_ref, lat_hbm, ada_hbm, qkv_hbm, out_hbm,
    updated_ref,
    lat, ada, wqkv, wout, normed, hidden, mods, gates, lat_rows, kv, queries, q_rows,
    acc, totals, attended,
    load_sem, mod_send, mod_recv, gate_send, gate_recv, row_send, row_recv,
    kv_send, kv_recv, q_send, q_recv, w_send, w_recv, att_send, att_recv,
):
    me = lax.axis_index("seq")
    part = lax.axis_index("tensor")
    pair = 2
    side = lax.rem(me, pair)
    rows, width = lat.shape
    columns = updated_ref.shape[1]
    head_size = q_gain_ref.shape[1]
    heads = queries.shape[1] // head_size

    def remote(src, dst, send, recv, axis, target):
        return pltpu.make_async_remote_copy(
            src_ref=src, dst_ref=dst, send_sem=send, recv_sem=recv,
            device_id={axis: target}, device_id_type=pl.DeviceIdType.MESH,
        )

    loads = [
        pltpu.make_async_copy(ada_hbm, ada, load_sem.at[0]),
        pltpu.make_async_copy(lat_hbm, lat, load_sem.at[1]),
        pltpu.make_async_copy(qkv_hbm.at[1], wqkv.at[1], load_sem.at[2]),
        pltpu.make_async_copy(qkv_hbm.at[2], wqkv.at[2], load_sem.at[3]),
        pltpu.make_async_copy(qkv_hbm.at[0], wqkv.at[0], load_sem.at[4]),
        pltpu.make_async_copy(
            out_hbm.at[:, pl.ds(pl.multiple_of(part * columns, 128), columns)],
            wout.at[part], load_sem.at[5],
        ),
    ]
    for load in loads:
        load.start()

    barrier = pltpu.get_barrier_semaphore()
    for step in range(1, parts):
        pl.semaphore_signal(
            barrier, inc=1, device_id={"tensor": lax.rem(part + step, parts)},
            device_id_type=pl.DeviceIdType.MESH,
        )

    @pl.loop(1, n)
    def _(step):
        pl.semaphore_signal(
            barrier, inc=1, device_id={"seq": lax.rem(me + step, n)},
            device_id_type=pl.DeviceIdType.MESH,
        )

    half_width = ada.shape[1] // 2
    order = lax.broadcasted_iota(jnp.int32, (16, half_width), 1).astype(F32)
    angles = level_ref[0].astype(F32) * jnp.exp(-math.log(10000.0) * order / half_width)
    waves = jnp.concatenate([jnp.cos(angles), jnp.sin(angles)], axis=1)
    emb = (waves * (1.0 / (1.0 + jnp.exp(-waves)))).astype(BF16)
    loads[0].wait()
    for j in range(2):
        mods[part, j : j + 1, :] = dot(emb, ada[j])[0:1]
    gates[me] = dot(emb, ada[2])[0:1]

    pl.semaphore_wait(barrier, n - 1 + parts - 1)

    def mod_copy(slot, target):
        return remote(
            mods.at[slot], mods.at[slot], mod_send.at[target], mod_recv.at[slot], "tensor", target
        )

    for step in range(1, parts):
        mod_copy(part, lax.rem(part + step, parts)).start()


    def slab_of(device):
        return pl.multiple_of((device * clean_rows) // slab * slab, slab)

    first_column = pl.multiple_of(part * columns, 128)

    def gate_copy(slot, target):
        return remote(
            gates.at[slot], gates.at[slot], gate_send.at[target], gate_recv.at[slot], "seq", target
        )

    def row_copy(slot, target):
        return remote(
            lat_hbm.at[pl.ds(slab_of(target), slab), pl.ds(first_column, columns)],
            lat_rows.at[slot], row_send.at[target], row_recv.at[slot], "seq", target,
        )

    def w_copy(slot, target):
        at = pl.ds(pl.multiple_of(target * columns, 128), columns)
        return remote(
            out_hbm.at[:, at], wout.at[slot], w_send.at[target], w_recv.at[slot], "tensor", target
        )

    @pl.loop(1, n)
    def _(step):
        target = lax.rem(me + step, n)
        gate_copy(me, target).start()
        row_copy(me, target).start()

    for step in range(1, parts):
        w_copy(part, lax.rem(part + step, parts)).start()

    loads[1].wait()
    own_slab = slab_of(me)
    lat_rows[me] = lat[pl.ds(own_slab, slab), pl.ds(first_column, columns)]

    tile = 16

    @pl.loop(0, rows // tile)
    def _(index):
        at = pl.ds(pl.multiple_of(index * tile, tile), tile)
        states = lat[at, :].astype(F32)
        centered = states - jnp.mean(states, axis=-1, keepdims=True)
        variance = jnp.mean(centered * centered, axis=-1, keepdims=True)
        normed[at, :] = centered * lax.rsqrt(variance + EPS)

    for step in range(1, parts):
        mod_copy(lax.rem(part + step, parts), part).wait_recv()
    for index in range(parts):
        at = slice(index * columns, (index + 1) * columns)
        hidden[:, at] = (
            normed[:, at] * (1.0 + mods[index, 1:2, :]) + mods[index, 0:1, :]
        ).astype(BF16)

    def scaled(matrix, gain, factor):
        power = jnp.mean(matrix * matrix, axis=-1, keepdims=True)
        return (matrix * lax.rsqrt(power + EPS) * gain * factor).astype(BF16)

    def kv_copy(kind, slot, way, target):
        return remote(
            kv.at[slot, kind], kv.at[slot, kind],
            kv_send.at[kind, way, slot], kv_recv.at[kind, slot], "seq", target,
        )

    def onward(kind, slot, way, act):
        target = (me - pair, me + pair, me + 1 - 2 * side)[way]
        there = (target >= 0, target < n, None)[way]
        run = functools.partial(act, kind, slot, way, target)
        if there is None:
            run()
        else:
            pl.when(there)(run)

    def start(kind, slot, way, target):
        kv_copy(kind, slot, way, target).start()

    def finish(kind, slot, way, target):
        kv_copy(kind, slot, way, target).wait_send()

    def spread_out(kind, slot):
        for way in range(3):
            onward(kind, slot, way, start)

    def q_copy(slot, target):
        return remote(
            queries.at[pl.ds(slab_of(target), slab), :], q_rows.at[slot],
            q_send.at[target], q_recv.at[slot], "seq", target,
        )

    def head_at(index):
        return slice(index * head_size, (index + 1) * head_size)

    loads[2].wait()
    raw = dot(hidden[...], wqkv[1])
    for h in range(heads):
        kv[me, 0, :, head_at(h)] = scaled(raw[:, head_at(h)], k_gain_ref[...], 1.0)

    spread_out(0, me)

    loads[3].wait()
    kv[me, 1] = dot(hidden[...], wqkv[2]).astype(BF16)

    spread_out(1, me)

    loads[4].wait()
    raw = dot(hidden[...], wqkv[0])
    for h in range(heads):
        queries[:, head_at(h)] = scaled(
            raw[:, head_at(h)], q_gain_ref[...], 1.0 / math.sqrt(head_size)
        )
    q_rows[me] = queries[pl.ds(own_slab, slab), :]

    @pl.loop(1, n)
    def _(step):
        target = lax.rem(me + step, n)
        q_copy(me, target).start()

    oldest = head_ref[0]
    own_rank = lax.rem(me - oldest + n, n)

    for h in range(heads):
        weights = jnp.exp(dot_t(queries[:, head_at(h)], kv[me, 0, :, head_at(h)]))
        totals[:, head_at(h)] = weights
        acc[:, head_at(h)] = dot(weights.astype(BF16), kv[me, 1, :, head_at(h)])

    def absorb(source):
        rank = lax.rem(source - oldest + n, n)
        seen = jnp.full((rows, rows), rank, jnp.int32) <= own_rank
        for h in range(heads):
            scores = dot_t(queries[:, head_at(h)], kv[source, 0, :, head_at(h)])
            weights = jnp.where(seen, jnp.exp(scores), 0.0)
            totals[:, head_at(h)] += weights
            acc[:, head_at(h)] += dot(weights.astype(BF16), kv[source, 1, :, head_at(h)])

    def take_across(source):
        kv_copy(0, source, 2, me).wait_recv()
        kv_copy(1, source, 2, me).wait_recv()
        absorb(source)

    other = me + 1 - 2 * side

    @pl.loop(1, n // pair)
    def _(step):
        below, above = me - step * pair, me + step * pair
        for kind in range(2):

            @pl.when(below >= 0)
            def _():
                kv_copy(kind, below, 1, me).wait_recv()
                onward(kind, below, 1, start)
                onward(kind, below, 2, start)

            @pl.when(above < n)
            def _():
                kv_copy(kind, above, 0, me).wait_recv()
                onward(kind, above, 0, start)
                onward(kind, above, 2, start)

        @pl.when(step == 1)
        def _():
            take_across(other)

        @pl.when((step > 1) & (other - (step - 1) * pair >= 0))
        def _():
            take_across(other - (step - 1) * pair)

        @pl.when((step > 1) & (other + (step - 1) * pair < n))
        def _():
            take_across(other + (step - 1) * pair)

        @pl.when(below >= 0)
        def _():
            absorb(below)

        @pl.when(above < n)
        def _():
            absorb(above)

    last = n - pair

    @pl.when(other - last >= 0)
    def _():
        take_across(other - last)

    @pl.when(other + last < n)
    def _():
        take_across(other + last)

    @pl.loop(1, n)
    def _(step):
        source = lax.rem(me - step + n, n)
        q_copy(source, me).wait_recv()
        gate_copy(source, me).wait_recv()
        row_copy(source, me).wait_recv()

    for h in range(heads):
        total = jnp.sum(totals[:, head_at(h)], axis=-1, keepdims=True)
        attended[part, 0:rows, head_at(h)] = (acc[:, head_at(h)] / total).astype(BF16)
        weights = jnp.exp(dot_t(q_rows[oldest, :, head_at(h)], kv[oldest, 0, :, head_at(h)]))
        total = jnp.sum(weights, axis=-1, keepdims=True)
        product = dot(weights.astype(BF16), kv[oldest, 1, :, head_at(h)])
        attended[part, rows:, head_at(h)] = (product / total).astype(BF16)

    core = lax.rem(part, 2)
    sibling = part + 1 - 2 * core

    def att_copy(slot, target, way):
        return remote(
            attended.at[slot], attended.at[slot], att_send.at[way], att_recv.at[slot],
            "tensor", target,
        )

    ahead = [lax.rem(part + 2 * step, parts) for step in range(1, parts // 2)]
    for way, target in enumerate(ahead):
        att_copy(part, target, way).start()
    att_copy(part, sibling, len(ahead)).start()

    loads[5].wait()
    total = dot(attended[part], wout[part])

    def add(slot, total):
        w_copy(slot, part).wait_recv()
        return total + dot(attended[slot], wout[slot])

    att_copy(sibling, part, 0).wait_recv()
    total = add(sibling, total)
    for way, slot in enumerate(ahead):
        att_copy(slot, part, 0).wait_recv()
        att_copy(slot, sibling, len(ahead) + 1 + way).start()
        total = add(slot, total)
    for slot in ahead:
        handed = slot + 1 - 2 * core
        att_copy(handed, part, 0).wait_recv()
        total = add(handed, total)

    own_states = lat[:, pl.ds(first_column, columns)].astype(F32)
    updated_ref[0:rows, :] = (own_states + gates[me] * total[0:rows]).astype(BF16)
    updated_ref[rows:, :] = (
        lat_rows[oldest].astype(F32) + gates[oldest] * total[rows:]
    ).astype(BF16)

    for way in range(parts - 1):
        att_copy(part, sibling, way).wait_send()
    for step in range(1, parts):
        target = lax.rem(part + step, parts)
        mod_copy(part, target).wait_send()
        w_copy(part, target).wait_send()

    @pl.loop(1, n)
    def _(step):
        target = lax.rem(me + step, n)
        q_copy(me, target).wait_send()
        gate_copy(me, target).wait_send()
        row_copy(me, target).wait_send()

    for kind in range(2):
        for way in range(3):
            onward(kind, me, way, finish)

    @pl.loop(1, n // pair)
    def _(step):
        below, above = me - step * pair, me + step * pair
        for kind in range(2):

            @pl.when(below >= 0)
            def _():
                onward(kind, below, 1, finish)
                onward(kind, below, 2, finish)

            @pl.when(above < n)
            def _():
                onward(kind, above, 0, finish)
                onward(kind, above, 2, finish)


def finish_kernel(n, head_ref, updated_ref, noise_ref, window_ref, clean_ref):
    rows = window_ref.shape[0]
    own_rank = lax.rem(lax.axis_index("seq") - head_ref[0] + n, n)
    leaving = jnp.full(window_ref.shape, own_rank, jnp.int32) == 0
    window_ref[...] = jnp.where(leaving, noise_ref[...], updated_ref[0:rows, :])
    clean_ref[...] = updated_ref[rows:, :]


def local(
    latents, levels, head_slot, fresh_noise, ada_weight, qkv_weight, q_gain, k_gain, out_weight
):
    n = lax.axis_size("seq")
    parts = lax.axis_size("tensor")
    rows, width = latents.shape
    columns = fresh_noise.shape[1]
    inner = out_weight.shape[0]
    clean_rows = rows // n
    slab = max(clean_rows, 16)
    vmem = pl.BlockSpec(memory_space=pltpu.VMEM)
    smem = pl.BlockSpec(memory_space=pltpu.SMEM)
    hbm = pl.BlockSpec(memory_space=pl.ANY)
    dma = pltpu.SemaphoreType.DMA
    updated = pl.pallas_call(
        functools.partial(kernel, n, parts, slab, clean_rows),
        out_shape=jax.ShapeDtypeStruct((rows + slab, columns), BF16),
        in_specs=[
            smem, smem, vmem, vmem, hbm, hbm, hbm, hbm,
        ],
        out_specs=vmem,
        scratch_shapes=[
            pltpu.VMEM((rows, width), BF16),
            pltpu.VMEM((3, ada_weight.shape[0], columns), BF16),
            pltpu.VMEM((3, width, inner), BF16),
            pltpu.VMEM((parts, inner, columns), BF16),
            pltpu.VMEM((rows, width), F32),
            pltpu.VMEM((rows, width), BF16),
            pltpu.VMEM((parts, 8, columns), F32),
            pltpu.VMEM((n, 1, columns), F32),
            pltpu.VMEM((n, slab, columns), BF16),
            pltpu.VMEM((n, 2, rows, inner), BF16),
            pltpu.VMEM((rows, inner), BF16),
            pltpu.VMEM((n, slab, inner), BF16),
            pltpu.VMEM((rows, inner), F32),
            pltpu.VMEM((rows, inner), F32),
            pltpu.VMEM((parts, rows + slab, inner), BF16),
            dma((6,)), dma((parts,)), dma((parts,)), dma((n,)), dma((n,)), dma((n,)), dma((n,)),
            dma((2, 3, n)), dma((2, n)), dma((n,)), dma((n,)), dma((parts,)), dma((parts,)),
            dma((parts,)), dma((parts,)),
        ],
        compiler_params=pltpu.CompilerParams(
            collective_id=0, has_side_effects=True, vmem_limit_bytes=60 * 1024 * 1024
        ),
    )(
        head_slot, levels, q_gain.reshape(1, -1), k_gain.reshape(1, -1), latents,
        jnp.transpose(ada_weight, (1, 0, 2)), jnp.transpose(qkv_weight, (1, 0, 2)), out_weight,
    )
    window, clean = pl.pallas_call(
        functools.partial(finish_kernel, n),
        out_shape=(
            jax.ShapeDtypeStruct((rows, columns), BF16),
            jax.ShapeDtypeStruct((slab, columns), BF16),
        ),
        in_specs=[smem, vmem, vmem],
        out_specs=(vmem, vmem),
    )(head_slot, updated, fresh_noise)
    if clean_rows < slab:
        start = (lax.axis_index("seq") * clean_rows) % slab
        clean = lax.dynamic_slice_in_dim(clean, start, clean_rows, 0)
    return window, clean


def solution(mesh):
    return jax.shard_map(
        local,
        mesh=mesh,
        in_specs=(
            P("seq", None),
            P("seq"),
            P(),
            P(None, "tensor"),
            P(None, None, "tensor"),
            P(None, None, "tensor"),
            P(),
            P(),
            P("tensor", None),
        ),
        out_specs=(P("seq", "tensor"), P("seq", "tensor")),
        check_vma=False,
    )
```

```python
import functools
import math

import jax
import jax.numpy as jnp
from jax import lax
from jax.experimental import pallas as pl
from jax.experimental.pallas import tpu as pltpu
from jax.sharding import PartitionSpec as P

F32 = jnp.float32
BF16 = jnp.bfloat16
EPS = 1e-06


def dot(a, b):
    return jnp.dot(a, b, preferred_element_type=F32)


def dot_t(a, b):
    return lax.dot_general(a, b, (((1,), (1,)), ((), ())), preferred_element_type=F32)


def kernel(
    n, parts, slab, clean_rows,
    head_hbm, level_hbm, q_gain_hbm, k_gain_hbm, noise_hbm, lat_hbm, ada_hbm, qkv_hbm, out_hbm,
    updated_ref,
    head_ref, level_ref, q_gain_ref, k_gain_ref, noise, lat, ada, wqkv, wout, normed, hidden, mods, gates, lat_rows, kv, queries, q_rows,
    acc, totals, attended,
    load_sem, mod_send, mod_recv, gate_send, gate_recv, row_send, row_recv,
    kv_send, kv_recv, q_send, q_recv, w_send, w_recv, att_send, att_recv,
):
    me = lax.axis_index("seq")
    part = lax.axis_index("tensor")
    pair = 2
    side = lax.rem(me, pair)
    rows, width = lat.shape
    columns = updated_ref.shape[1]
    head_size = q_gain_ref.shape[1]
    heads = queries.shape[1] // head_size

    def remote(src, dst, send, recv, axis, target):
        return pltpu.make_async_remote_copy(
            src_ref=src, dst_ref=dst, send_sem=send, recv_sem=recv,
            device_id={axis: target}, device_id_type=pl.DeviceIdType.MESH,
        )

    loads = [
        pltpu.make_async_copy(ada_hbm, ada, load_sem.at[0]),
        pltpu.make_async_copy(lat_hbm, lat, load_sem.at[1]),
        pltpu.make_async_copy(qkv_hbm.at[1], wqkv.at[1], load_sem.at[2]),
        pltpu.make_async_copy(qkv_hbm.at[2], wqkv.at[2], load_sem.at[3]),
        pltpu.make_async_copy(qkv_hbm.at[0], wqkv.at[0], load_sem.at[4]),
        pltpu.make_async_copy(
            out_hbm.at[:, pl.ds(pl.multiple_of(part * columns, 128), columns)],
            wout.at[part], load_sem.at[5],
        ),
        pltpu.make_async_copy(noise_hbm, noise, load_sem.at[6]),
    ]
    small = [
        pltpu.make_async_copy(source, held, load_sem.at[7 + index])
        for index, (source, held) in enumerate((
            (level_hbm, level_ref), (head_hbm, head_ref),
            (q_gain_hbm, q_gain_ref), (k_gain_hbm, k_gain_ref),
        ))
    ]
    for load in small:
        load.start()
    for load in loads:
        load.start()

    barrier = pltpu.get_barrier_semaphore()
    for step in range(1, parts):
        pl.semaphore_signal(
            barrier, inc=1, device_id={"tensor": lax.rem(part + step, parts)},
            device_id_type=pl.DeviceIdType.MESH,
        )

    @pl.loop(1, n)
    def _(step):
        pl.semaphore_signal(
            barrier, inc=1, device_id={"seq": lax.rem(me + step, n)},
            device_id_type=pl.DeviceIdType.MESH,
        )

    for load in small:
        load.wait()
    half_width = ada.shape[1] // 2
    order = lax.broadcasted_iota(jnp.int32, (16, half_width), 1).astype(F32)
    angles = level_ref[0].astype(F32) * jnp.exp(-math.log(10000.0) * order / half_width)
    waves = jnp.concatenate([jnp.cos(angles), jnp.sin(angles)], axis=1)
    emb = (waves * (1.0 / (1.0 + jnp.exp(-waves)))).astype(BF16)
    loads[0].wait()
    for j in range(2):
        mods[part, j : j + 1, :] = dot(emb, ada[j])[0:1]
    gates[me] = dot(emb, ada[2])[0:1]

    pl.semaphore_wait(barrier, n - 1 + parts - 1)

    def mod_copy(slot, target):
        return remote(
            mods.at[slot], mods.at[slot], mod_send.at[target], mod_recv.at[slot], "tensor", target
        )

    for step in range(1, parts):
        mod_copy(part, lax.rem(part + step, parts)).start()


    def slab_of(device):
        return pl.multiple_of((device * clean_rows) // slab * slab, slab)

    first_column = pl.multiple_of(part * columns, 128)

    def gate_copy(slot, target):
        return remote(
            gates.at[slot], gates.at[slot], gate_send.at[target], gate_recv.at[slot], "seq", target
        )

    def row_copy(slot, target):
        return remote(
            lat_hbm.at[pl.ds(slab_of(target), slab), pl.ds(first_column, columns)],
            lat_rows.at[slot], row_send.at[target], row_recv.at[slot], "seq", target,
        )

    def w_copy(slot, target):
        at = pl.ds(pl.multiple_of(target * columns, 128), columns)
        return remote(
            out_hbm.at[:, at], wout.at[slot], w_send.at[target], w_recv.at[slot], "tensor", target
        )

    @pl.loop(1, n)
    def _(step):
        target = lax.rem(me + step, n)
        gate_copy(me, target).start()
        row_copy(me, target).start()

    for step in range(1, parts):
        w_copy(part, lax.rem(part + step, parts)).start()

    loads[1].wait()
    own_slab = slab_of(me)
    lat_rows[me] = lat[pl.ds(own_slab, slab), pl.ds(first_column, columns)]

    tile = 16

    @pl.loop(0, rows // tile)
    def _(index):
        at = pl.ds(pl.multiple_of(index * tile, tile), tile)
        states = lat[at, :].astype(F32)
        centered = states - jnp.mean(states, axis=-1, keepdims=True)
        variance = jnp.mean(centered * centered, axis=-1, keepdims=True)
        normed[at, :] = centered * lax.rsqrt(variance + EPS)

    for step in range(1, parts):
        mod_copy(lax.rem(part + step, parts), part).wait_recv()
    for index in range(parts):
        at = slice(index * columns, (index + 1) * columns)
        hidden[:, at] = (
            normed[:, at] * (1.0 + mods[index, 1:2, :]) + mods[index, 0:1, :]
        ).astype(BF16)

    def scaled(matrix, gain, factor):
        power = jnp.mean(matrix * matrix, axis=-1, keepdims=True)
        return (matrix * lax.rsqrt(power + EPS) * gain * factor).astype(BF16)

    def kv_copy(kind, slot, way, target):
        return remote(
            kv.at[slot, kind], kv.at[slot, kind],
            kv_send.at[kind, way, slot], kv_recv.at[kind, slot], "seq", target,
        )

    def onward(kind, slot, way, act):
        target = (me - pair, me + pair, me + 1 - 2 * side)[way]
        there = (target >= 0, target < n, None)[way]
        run = functools.partial(act, kind, slot, way, target)
        if there is None:
            run()
        else:
            pl.when(there)(run)

    def start(kind, slot, way, target):
        kv_copy(kind, slot, way, target).start()

    def finish(kind, slot, way, target):
        kv_copy(kind, slot, way, target).wait_send()

    def spread_out(kind, slot):
        for way in range(3):
            onward(kind, slot, way, start)

    def q_copy(slot, target):
        return remote(
            queries.at[pl.ds(slab_of(target), slab), :], q_rows.at[slot],
            q_send.at[target], q_recv.at[slot], "seq", target,
        )

    def head_at(index):
        return slice(index * head_size, (index + 1) * head_size)

    loads[2].wait()
    raw = dot(hidden[...], wqkv[1])
    for h in range(heads):
        kv[me, 0, :, head_at(h)] = scaled(raw[:, head_at(h)], k_gain_ref[...], 1.0)

    spread_out(0, me)

    loads[3].wait()
    kv[me, 1] = dot(hidden[...], wqkv[2]).astype(BF16)

    spread_out(1, me)

    loads[4].wait()
    raw = dot(hidden[...], wqkv[0])
    for h in range(heads):
        queries[:, head_at(h)] = scaled(
            raw[:, head_at(h)], q_gain_ref[...], 1.0 / math.sqrt(head_size)
        )
    q_rows[me] = queries[pl.ds(own_slab, slab), :]

    @pl.loop(1, n)
    def _(step):
        target = lax.rem(me + step, n)
        q_copy(me, target).start()

    oldest = head_ref[0]
    own_rank = lax.rem(me - oldest + n, n)

    for h in range(heads):
        weights = jnp.exp(dot_t(queries[:, head_at(h)], kv[me, 0, :, head_at(h)]))
        totals[:, head_at(h)] = weights
        acc[:, head_at(h)] = dot(weights.astype(BF16), kv[me, 1, :, head_at(h)])

    def absorb(source):
        rank = lax.rem(source - oldest + n, n)
        seen = jnp.full((rows, rows), rank, jnp.int32) <= own_rank
        for h in range(heads):
            scores = dot_t(queries[:, head_at(h)], kv[source, 0, :, head_at(h)])
            weights = jnp.where(seen, jnp.exp(scores), 0.0)
            totals[:, head_at(h)] += weights
            acc[:, head_at(h)] += dot(weights.astype(BF16), kv[source, 1, :, head_at(h)])

    def take_across(source):
        kv_copy(0, source, 2, me).wait_recv()
        kv_copy(1, source, 2, me).wait_recv()
        absorb(source)

    other = me + 1 - 2 * side

    @pl.loop(1, n // pair)
    def _(step):
        below, above = me - step * pair, me + step * pair
        for kind in range(2):

            @pl.when(below >= 0)
            def _():
                kv_copy(kind, below, 1, me).wait_recv()
                onward(kind, below, 1, start)
                onward(kind, below, 2, start)

            @pl.when(above < n)
            def _():
                kv_copy(kind, above, 0, me).wait_recv()
                onward(kind, above, 0, start)
                onward(kind, above, 2, start)

        @pl.when(step == 1)
        def _():
            take_across(other)

        @pl.when((step > 1) & (other - (step - 1) * pair >= 0))
        def _():
            take_across(other - (step - 1) * pair)

        @pl.when((step > 1) & (other + (step - 1) * pair < n))
        def _():
            take_across(other + (step - 1) * pair)

        @pl.when(below >= 0)
        def _():
            absorb(below)

        @pl.when(above < n)
        def _():
            absorb(above)

    last = n - pair

    @pl.when(other - last >= 0)
    def _():
        take_across(other - last)

    @pl.when(other + last < n)
    def _():
        take_across(other + last)

    @pl.loop(1, n)
    def _(step):
        source = lax.rem(me - step + n, n)
        q_copy(source, me).wait_recv()
        gate_copy(source, me).wait_recv()
        row_copy(source, me).wait_recv()

    for h in range(heads):
        total = jnp.sum(totals[:, head_at(h)], axis=-1, keepdims=True)
        attended[part, 0:rows, head_at(h)] = (acc[:, head_at(h)] / total).astype(BF16)
        weights = jnp.exp(dot_t(q_rows[oldest, :, head_at(h)], kv[oldest, 0, :, head_at(h)]))
        total = jnp.sum(weights, axis=-1, keepdims=True)
        product = dot(weights.astype(BF16), kv[oldest, 1, :, head_at(h)])
        attended[part, rows:, head_at(h)] = (product / total).astype(BF16)

    core = lax.rem(part, 2)
    sibling = part + 1 - 2 * core

    def att_copy(slot, target, way):
        return remote(
            attended.at[slot], attended.at[slot], att_send.at[way], att_recv.at[slot],
            "tensor", target,
        )

    ahead = [lax.rem(part + 2 * step, parts) for step in range(1, parts // 2)]
    for way, target in enumerate(ahead):
        att_copy(part, target, way).start()
    att_copy(part, sibling, len(ahead)).start()

    loads[5].wait()
    total = dot(attended[part], wout[part])

    def add(slot, total):
        w_copy(slot, part).wait_recv()
        return total + dot(attended[slot], wout[slot])

    att_copy(sibling, part, 0).wait_recv()
    total = add(sibling, total)
    for way, slot in enumerate(ahead):
        att_copy(slot, part, 0).wait_recv()
        att_copy(slot, sibling, len(ahead) + 1 + way).start()
        total = add(slot, total)
    for slot in ahead:
        handed = slot + 1 - 2 * core
        att_copy(handed, part, 0).wait_recv()
        total = add(handed, total)

    own_states = lat[:, pl.ds(first_column, columns)].astype(F32)
    updated = (own_states + gates[me] * total[0:rows]).astype(BF16)
    leaving = jnp.full((rows, columns), own_rank, jnp.int32) == 0
    loads[6].wait()
    updated_ref[0:rows, :] = jnp.where(leaving, noise[...], updated)
    updated_ref[rows:, :] = (
        lat_rows[oldest].astype(F32) + gates[oldest] * total[rows:]
    ).astype(BF16)

    for way in range(parts - 1):
        att_copy(part, sibling, way).wait_send()
    for step in range(1, parts):
        target = lax.rem(part + step, parts)
        mod_copy(part, target).wait_send()
        w_copy(part, target).wait_send()

    @pl.loop(1, n)
    def _(step):
        target = lax.rem(me + step, n)
        q_copy(me, target).wait_send()
        gate_copy(me, target).wait_send()
        row_copy(me, target).wait_send()

    for kind in range(2):
        for way in range(3):
            onward(kind, me, way, finish)

    @pl.loop(1, n // pair)
    def _(step):
        below, above = me - step * pair, me + step * pair
        for kind in range(2):

            @pl.when(below >= 0)
            def _():
                onward(kind, below, 1, finish)
                onward(kind, below, 2, finish)

            @pl.when(above < n)
            def _():
                onward(kind, above, 0, finish)
                onward(kind, above, 2, finish)


def finish_kernel(updated_ref, window_ref, clean_ref):
    rows = window_ref.shape[0]
    window_ref[...] = updated_ref[0:rows, :]
    clean_ref[...] = updated_ref[rows:, :]


def local(
    latents, levels, head_slot, fresh_noise, ada_weight, qkv_weight, q_gain, k_gain, out_weight
):
    n = lax.axis_size("seq")
    parts = lax.axis_size("tensor")
    rows, width = latents.shape
    columns = fresh_noise.shape[1]
    inner = out_weight.shape[0]
    clean_rows = rows // n
    slab = max(clean_rows, 16)
    vmem = pl.BlockSpec(memory_space=pltpu.VMEM)
    hbm = pl.BlockSpec(memory_space=pltpu.HBM)
    dma = pltpu.SemaphoreType.DMA
    updated = pl.pallas_call(
        functools.partial(kernel, n, parts, slab, clean_rows),
        out_shape=jax.ShapeDtypeStruct((rows + slab, columns), BF16),
        in_specs=[
            hbm, hbm, hbm, hbm, hbm, hbm, hbm, hbm, hbm,
        ],
        out_specs=vmem,
        scratch_shapes=[
            pltpu.SMEM((1,), jnp.int32),
            pltpu.SMEM((1,), jnp.int32),
            pltpu.VMEM((1, q_gain.shape[0]), F32),
            pltpu.VMEM((1, q_gain.shape[0]), F32),
            pltpu.VMEM((rows, columns), BF16),
            pltpu.VMEM((rows, width), BF16),
            pltpu.VMEM((3, ada_weight.shape[0], columns), BF16),
            pltpu.VMEM((3, width, inner), BF16),
            pltpu.VMEM((parts, inner, columns), BF16),
            pltpu.VMEM((rows, width), F32),
            pltpu.VMEM((rows, width), BF16),
            pltpu.VMEM((parts, 8, columns), F32),
            pltpu.VMEM((n, 1, columns), F32),
            pltpu.VMEM((n, slab, columns), BF16),
            pltpu.VMEM((n, 2, rows, inner), BF16),
            pltpu.VMEM((rows, inner), BF16),
            pltpu.VMEM((n, slab, inner), BF16),
            pltpu.VMEM((rows, inner), F32),
            pltpu.VMEM((rows, inner), F32),
            pltpu.VMEM((parts, rows + slab, inner), BF16),
            dma((11,)), dma((parts,)), dma((parts,)), dma((n,)), dma((n,)), dma((n,)), dma((n,)),
            dma((2, 3, n)), dma((2, n)), dma((n,)), dma((n,)), dma((parts,)), dma((parts,)),
            dma((parts,)), dma((parts,)),
        ],
        compiler_params=pltpu.CompilerParams(
            collective_id=0, has_side_effects=True, vmem_limit_bytes=60 * 1024 * 1024
        ),
    )(
        head_slot, levels, q_gain.reshape(1, -1), k_gain.reshape(1, -1), fresh_noise, latents,
        jnp.transpose(ada_weight, (1, 0, 2)), jnp.transpose(qkv_weight, (1, 0, 2)), out_weight,
    )
    window, clean = pl.pallas_call(
        finish_kernel,
        out_shape=(
            jax.ShapeDtypeStruct((rows, columns), BF16),
            jax.ShapeDtypeStruct((slab, columns), BF16),
        ),
        in_specs=[vmem],
        out_specs=(vmem, vmem),
    )(updated)
    if clean_rows < slab:
        start = (lax.axis_index("seq") * clean_rows) % slab
        clean = lax.dynamic_slice_in_dim(clean, start, clean_rows, 0)
    return window, clean


def solution(mesh):
    return jax.shard_map(
        local,
        mesh=mesh,
        in_specs=(
            P("seq", None),
            P("seq"),
            P(),
            P(None, "tensor"),
            P(None, None, "tensor"),
            P(None, None, "tensor"),
            P(),
            P(),
            P("tensor", None),
        ),
        out_specs=(P("seq", "tensor"), P("seq", "tensor")),
        check_vma=False,
    )
```

```python
import functools
import math

import jax
import jax.numpy as jnp
from jax import lax
from jax.experimental import pallas as pl
from jax.experimental.pallas import tpu as pltpu
from jax.sharding import PartitionSpec as P

F32 = jnp.float32
BF16 = jnp.bfloat16
EPS = 1e-06


def dot(a, b):
    return jnp.dot(a, b, preferred_element_type=F32)


def dot_t(a, b):
    return lax.dot_general(a, b, (((1,), (1,)), ((), ())), preferred_element_type=F32)


def kernel(
    n, parts, slab, clean_rows,
    head_hbm, level_hbm, q_gain_hbm, k_gain_hbm, noise_hbm, lat_hbm, ada_hbm, qkv_hbm, out_hbm,
    updated_ref,
    head_ref, level_ref, q_gain_ref, k_gain_ref, noise, lat, ada, wqkv, wout, normed, hidden, mods, gates, lat_rows, kv, queries, q_rows,
    acc, totals, attended,
    load_sem, mod_send, mod_recv, gate_send, gate_recv, row_send, row_recv,
    kv_send, kv_recv, q_send, q_recv, w_send, w_recv, att_send, att_recv,
):
    me = lax.axis_index("seq")
    part = lax.axis_index("tensor")
    pair = 2
    side = lax.rem(me, pair)
    mate = me + pair * (1 - 2 * lax.rem(me // pair, 2))
    rows, width = lat.shape
    columns = updated_ref.shape[1]
    head_size = q_gain_ref.shape[1]
    heads = queries.shape[1] // head_size

    def remote(src, dst, send, recv, axis, target):
        return pltpu.make_async_remote_copy(
            src_ref=src, dst_ref=dst, send_sem=send, recv_sem=recv,
            device_id={axis: target}, device_id_type=pl.DeviceIdType.MESH,
        )

    loads = [
        pltpu.make_async_copy(ada_hbm, ada, load_sem.at[0]),
        pltpu.make_async_copy(lat_hbm, lat, load_sem.at[1]),
        pltpu.make_async_copy(qkv_hbm.at[1], wqkv.at[1], load_sem.at[2]),
        pltpu.make_async_copy(qkv_hbm.at[2], wqkv.at[2], load_sem.at[3]),
        pltpu.make_async_copy(qkv_hbm.at[0], wqkv.at[0], load_sem.at[4]),
        pltpu.make_async_copy(
            out_hbm.at[:, pl.ds(pl.multiple_of(part * columns, 128), columns)],
            wout.at[part], load_sem.at[5],
        ),
        pltpu.make_async_copy(noise_hbm, noise, load_sem.at[6]),
    ]
    small = [
        pltpu.make_async_copy(source, held, load_sem.at[7 + index])
        for index, (source, held) in enumerate((
            (level_hbm, level_ref), (head_hbm, head_ref),
            (q_gain_hbm, q_gain_ref), (k_gain_hbm, k_gain_ref),
        ))
    ]
    for load in small:
        load.start()
    for load in loads:
        load.start()

    barrier = pltpu.get_barrier_semaphore()
    for step in range(1, parts):
        pl.semaphore_signal(
            barrier, inc=1, device_id={"tensor": lax.rem(part + step, parts)},
            device_id_type=pl.DeviceIdType.MESH,
        )

    @pl.loop(1, n)
    def _(step):
        pl.semaphore_signal(
            barrier, inc=1, device_id={"seq": lax.rem(me + step, n)},
            device_id_type=pl.DeviceIdType.MESH,
        )

    for load in small:
        load.wait()
    half_width = ada.shape[1] // 2
    order = lax.broadcasted_iota(jnp.int32, (16, half_width), 1).astype(F32)
    angles = level_ref[0].astype(F32) * jnp.exp(-math.log(10000.0) * order / half_width)
    waves = jnp.concatenate([jnp.cos(angles), jnp.sin(angles)], axis=1)
    emb = (waves * (1.0 / (1.0 + jnp.exp(-waves)))).astype(BF16)
    loads[0].wait()
    for j in range(2):
        mods[part, j : j + 1, :] = dot(emb, ada[j])[0:1]
    gates[me] = dot(emb, ada[2])[0:1]

    pl.semaphore_wait(barrier, n - 1 + parts - 1)

    def mod_copy(slot, target):
        return remote(
            mods.at[slot], mods.at[slot], mod_send.at[target], mod_recv.at[slot], "tensor", target
        )

    for step in range(1, parts):
        mod_copy(part, lax.rem(part + step, parts)).start()


    def slab_of(device):
        return pl.multiple_of((device * clean_rows) // slab * slab, slab)

    first_column = pl.multiple_of(part * columns, 128)

    def gate_copy(slot, target):
        return remote(
            gates.at[slot], gates.at[slot], gate_send.at[target], gate_recv.at[slot], "seq", target
        )

    def row_copy(slot, target):
        return remote(
            lat_hbm.at[pl.ds(slab_of(target), slab), pl.ds(first_column, columns)],
            lat_rows.at[slot], row_send.at[target], row_recv.at[slot], "seq", target,
        )

    def w_copy(slot, target):
        at = pl.ds(pl.multiple_of(target * columns, 128), columns)
        return remote(
            out_hbm.at[:, at], wout.at[slot], w_send.at[target], w_recv.at[slot], "tensor", target
        )

    @pl.loop(1, n)
    def _(step):
        target = lax.rem(me + step, n)
        gate_copy(me, target).start()
        row_copy(me, target).start()

    for step in range(1, parts):
        w_copy(part, lax.rem(part + step, parts)).start()

    loads[1].wait()
    own_slab = slab_of(me)
    lat_rows[me] = lat[pl.ds(own_slab, slab), pl.ds(first_column, columns)]

    tile = 16

    @pl.loop(0, rows // tile)
    def _(index):
        at = pl.ds(pl.multiple_of(index * tile, tile), tile)
        states = lat[at, :].astype(F32)
        centered = states - jnp.mean(states, axis=-1, keepdims=True)
        variance = jnp.mean(centered * centered, axis=-1, keepdims=True)
        normed[at, :] = centered * lax.rsqrt(variance + EPS)

    for step in range(1, parts):
        mod_copy(lax.rem(part + step, parts), part).wait_recv()
    for index in range(parts):
        at = slice(index * columns, (index + 1) * columns)
        hidden[:, at] = (
            normed[:, at] * (1.0 + mods[index, 1:2, :]) + mods[index, 0:1, :]
        ).astype(BF16)

    def scaled(matrix, gain, factor):
        power = jnp.mean(matrix * matrix, axis=-1, keepdims=True)
        return (matrix * lax.rsqrt(power + EPS) * gain * factor).astype(BF16)

    def kv_copy(kind, slot, way, target):
        return remote(
            kv.at[slot, kind], kv.at[slot, kind],
            kv_send.at[kind, way, slot], kv_recv.at[kind, slot], "seq", target,
        )

    def onward(kind, slot, way, act):
        target = (me - pair, me + pair, me + 1 - 2 * side)[way]
        there = (target >= 0, target < n, None)[way]
        run = functools.partial(act, kind, slot, way, target)
        if there is None:
            run()
        else:
            pl.when(there)(run)

    def hand_across(kind, slot, act):
        if kind == 0:
            onward(kind, slot, 2, act)
        else:
            pl.when(slot != mate)(lambda: onward(kind, slot, 2, act))

    def start(kind, slot, way, target):
        kv_copy(kind, slot, way, target).start()

    def finish(kind, slot, way, target):
        kv_copy(kind, slot, way, target).wait_send()

    def spread_out(kind, slot):
        for way in range(3):
            onward(kind, slot, way, start)

    def q_copy(slot, target):
        return remote(
            queries.at[pl.ds(slab_of(target), slab), :], q_rows.at[slot],
            q_send.at[target], q_recv.at[slot], "seq", target,
        )

    def head_at(index):
        return slice(index * head_size, (index + 1) * head_size)

    loads[2].wait()
    raw = dot(hidden[...], wqkv[1])
    for h in range(heads):
        kv[me, 0, :, head_at(h)] = scaled(raw[:, head_at(h)], k_gain_ref[...], 1.0)

    spread_out(0, me)

    loads[3].wait()
    kv[me, 1] = dot(hidden[...], wqkv[2]).astype(BF16)

    spread_out(1, me)

    loads[4].wait()
    raw = dot(hidden[...], wqkv[0])
    for h in range(heads):
        queries[:, head_at(h)] = scaled(
            raw[:, head_at(h)], q_gain_ref[...], 1.0 / math.sqrt(head_size)
        )
    q_rows[me] = queries[pl.ds(own_slab, slab), :]

    @pl.loop(1, n)
    def _(step):
        target = lax.rem(me + step, n)
        q_copy(me, target).start()

    oldest = head_ref[0]
    own_rank = lax.rem(me - oldest + n, n)

    for h in range(heads):
        weights = jnp.exp(dot_t(queries[:, head_at(h)], kv[me, 0, :, head_at(h)]))
        totals[:, head_at(h)] = weights
        acc[:, head_at(h)] = dot(weights.astype(BF16), kv[me, 1, :, head_at(h)])

    def absorb(source):
        rank = lax.rem(source - oldest + n, n)
        seen = jnp.full((rows, rows), rank, jnp.int32) <= own_rank
        for h in range(heads):
            scores = dot_t(queries[:, head_at(h)], kv[source, 0, :, head_at(h)])
            weights = jnp.where(seen, jnp.exp(scores), 0.0)
            totals[:, head_at(h)] += weights
            acc[:, head_at(h)] += dot(weights.astype(BF16), kv[source, 1, :, head_at(h)])

    def take_across(source):
        kv_copy(0, source, 2, me).wait_recv()
        kv_copy(1, source, 2, me).wait_recv()
        absorb(source)

    other = me + 1 - 2 * side

    @pl.loop(1, n // pair)
    def _(step):
        below, above = me - step * pair, me + step * pair
        for kind in range(2):

            @pl.when(below >= 0)
            def _():
                kv_copy(kind, below, 1, me).wait_recv()
                onward(kind, below, 1, start)
                hand_across(kind, below, start)

            @pl.when(above < n)
            def _():
                kv_copy(kind, above, 0, me).wait_recv()
                onward(kind, above, 0, start)
                hand_across(kind, above, start)

        @pl.when(step == 1)
        def _():
            kv_copy(1, other, 0, me).wait_recv()
            kv_copy(1, other, 0, mate).start()
            kv_copy(0, other, 2, me).wait_recv()
            absorb(other)

        @pl.when((step > 1) & (other - (step - 1) * pair >= 0))
        def _():
            take_across(other - (step - 1) * pair)

        @pl.when((step > 1) & (other + (step - 1) * pair < n))
        def _():
            take_across(other + (step - 1) * pair)

        @pl.when(below >= 0)
        def _():
            absorb(below)

        @pl.when(above < n)
        def _():
            absorb(above)

    last = n - pair

    @pl.when(other - last >= 0)
    def _():
        take_across(other - last)

    @pl.when(other + last < n)
    def _():
        take_across(other + last)

    @pl.loop(1, n)
    def _(step):
        source = lax.rem(me - step + n, n)
        q_copy(source, me).wait_recv()
        gate_copy(source, me).wait_recv()
        row_copy(source, me).wait_recv()

    for h in range(heads):
        total = jnp.sum(totals[:, head_at(h)], axis=-1, keepdims=True)
        attended[part, 0:rows, head_at(h)] = (acc[:, head_at(h)] / total).astype(BF16)
        weights = jnp.exp(dot_t(q_rows[oldest, :, head_at(h)], kv[oldest, 0, :, head_at(h)]))
        total = jnp.sum(weights, axis=-1, keepdims=True)
        product = dot(weights.astype(BF16), kv[oldest, 1, :, head_at(h)])
        attended[part, rows:, head_at(h)] = (product / total).astype(BF16)

    core = lax.rem(part, 2)
    sibling = part + 1 - 2 * core

    def att_copy(slot, target, way):
        return remote(
            attended.at[slot], attended.at[slot], att_send.at[way], att_recv.at[slot],
            "tensor", target,
        )

    ahead = [lax.rem(part + 2 * step, parts) for step in range(1, parts // 2)]
    for way, target in enumerate(ahead):
        att_copy(part, target, way).start()
    att_copy(part, sibling, len(ahead)).start()

    loads[5].wait()
    total = dot(attended[part], wout[part])

    def add(slot, total):
        w_copy(slot, part).wait_recv()
        return total + dot(attended[slot], wout[slot])

    att_copy(sibling, part, 0).wait_recv()
    total = add(sibling, total)
    for way, slot in enumerate(ahead):
        att_copy(slot, part, 0).wait_recv()
        att_copy(slot, sibling, len(ahead) + 1 + way).start()
        total = add(slot, total)
    for slot in ahead:
        handed = slot + 1 - 2 * core
        att_copy(handed, part, 0).wait_recv()
        total = add(handed, total)

    own_states = lat[:, pl.ds(first_column, columns)].astype(F32)
    updated = (own_states + gates[me] * total[0:rows]).astype(BF16)
    leaving = jnp.full((rows, columns), own_rank, jnp.int32) == 0
    loads[6].wait()
    updated_ref[0:rows, :] = jnp.where(leaving, noise[...], updated)
    updated_ref[rows:, :] = (
        lat_rows[oldest].astype(F32) + gates[oldest] * total[rows:]
    ).astype(BF16)

    for way in range(parts - 1):
        att_copy(part, sibling, way).wait_send()
    for step in range(1, parts):
        target = lax.rem(part + step, parts)
        mod_copy(part, target).wait_send()
        w_copy(part, target).wait_send()

    @pl.loop(1, n)
    def _(step):
        target = lax.rem(me + step, n)
        q_copy(me, target).wait_send()
        gate_copy(me, target).wait_send()
        row_copy(me, target).wait_send()

    kv_copy(1, other, 0, mate).wait_send()
    for kind in range(2):
        for way in range(3):
            onward(kind, me, way, finish)

    @pl.loop(1, n // pair)
    def _(step):
        below, above = me - step * pair, me + step * pair
        for kind in range(2):

            @pl.when(below >= 0)
            def _():
                onward(kind, below, 1, finish)
                hand_across(kind, below, finish)

            @pl.when(above < n)
            def _():
                onward(kind, above, 0, finish)
                hand_across(kind, above, finish)


def finish_kernel(updated_ref, window_ref, clean_ref):
    rows = window_ref.shape[0]
    window_ref[...] = updated_ref[0:rows, :]
    clean_ref[...] = updated_ref[rows:, :]


def local(
    latents, levels, head_slot, fresh_noise, ada_weight, qkv_weight, q_gain, k_gain, out_weight
):
    n = lax.axis_size("seq")
    parts = lax.axis_size("tensor")
    rows, width = latents.shape
    columns = fresh_noise.shape[1]
    inner = out_weight.shape[0]
    clean_rows = rows // n
    slab = max(clean_rows, 16)
    vmem = pl.BlockSpec(memory_space=pltpu.VMEM)
    hbm = pl.BlockSpec(memory_space=pltpu.HBM)
    dma = pltpu.SemaphoreType.DMA
    updated = pl.pallas_call(
        functools.partial(kernel, n, parts, slab, clean_rows),
        out_shape=jax.ShapeDtypeStruct((rows + slab, columns), BF16),
        in_specs=[
            hbm, hbm, hbm, hbm, hbm, hbm, hbm, hbm, hbm,
        ],
        out_specs=vmem,
        scratch_shapes=[
            pltpu.SMEM((1,), jnp.int32),
            pltpu.SMEM((1,), jnp.int32),
            pltpu.VMEM((1, q_gain.shape[0]), F32),
            pltpu.VMEM((1, q_gain.shape[0]), F32),
            pltpu.VMEM((rows, columns), BF16),
            pltpu.VMEM((rows, width), BF16),
            pltpu.VMEM((3, ada_weight.shape[0], columns), BF16),
            pltpu.VMEM((3, width, inner), BF16),
            pltpu.VMEM((parts, inner, columns), BF16),
            pltpu.VMEM((rows, width), F32),
            pltpu.VMEM((rows, width), BF16),
            pltpu.VMEM((parts, 8, columns), F32),
            pltpu.VMEM((n, 1, columns), F32),
            pltpu.VMEM((n, slab, columns), BF16),
            pltpu.VMEM((n, 2, rows, inner), BF16),
            pltpu.VMEM((rows, inner), BF16),
            pltpu.VMEM((n, slab, inner), BF16),
            pltpu.VMEM((rows, inner), F32),
            pltpu.VMEM((rows, inner), F32),
            pltpu.VMEM((parts, rows + slab, inner), BF16),
            dma((11,)), dma((parts,)), dma((parts,)), dma((n,)), dma((n,)), dma((n,)), dma((n,)),
            dma((2, 3, n)), dma((2, n)), dma((n,)), dma((n,)), dma((parts,)), dma((parts,)),
            dma((parts,)), dma((parts,)),
        ],
        compiler_params=pltpu.CompilerParams(
            collective_id=0, has_side_effects=True, vmem_limit_bytes=60 * 1024 * 1024
        ),
    )(
        head_slot, levels, q_gain.reshape(1, -1), k_gain.reshape(1, -1), fresh_noise, latents,
        jnp.transpose(ada_weight, (1, 0, 2)), jnp.transpose(qkv_weight, (1, 0, 2)), out_weight,
    )
    window, clean = pl.pallas_call(
        finish_kernel,
        out_shape=(
            jax.ShapeDtypeStruct((rows, columns), BF16),
            jax.ShapeDtypeStruct((slab, columns), BF16),
        ),
        in_specs=[vmem],
        out_specs=(vmem, vmem),
    )(updated)
    if clean_rows < slab:
        start = (lax.axis_index("seq") * clean_rows) % slab
        clean = lax.dynamic_slice_in_dim(clean, start, clean_rows, 0)
    return window, clean


def solution(mesh):
    return jax.shard_map(
        local,
        mesh=mesh,
        in_specs=(
            P("seq", None),
            P("seq"),
            P(),
            P(None, "tensor"),
            P(None, None, "tensor"),
            P(None, None, "tensor"),
            P(),
            P(),
            P("tensor", None),
        ),
        out_specs=(P("seq", "tensor"), P("seq", "tensor")),
        check_vma=False,
    )
```

```python
import functools
import math

import jax
import jax.numpy as jnp
from jax import lax
from jax.experimental import pallas as pl
from jax.experimental.pallas import tpu as pltpu
from jax.sharding import PartitionSpec as P

F32 = jnp.float32
BF16 = jnp.bfloat16
EPS = 1e-06


def dot(a, b):
    return jnp.dot(a, b, preferred_element_type=F32)


def dot_t(a, b):
    return lax.dot_general(a, b, (((1,), (1,)), ((), ())), preferred_element_type=F32)


def kernel(
    n, parts, slab, clean_rows,
    head_hbm, level_hbm, q_gain_hbm, k_gain_hbm, noise_hbm, lat_hbm, ada_hbm, qkv_hbm, out_hbm,
    updated_ref,
    head_ref, level_ref, q_gain_ref, k_gain_ref, noise, lat, ada, wqkv, wout, normed, hidden, mods, gates, lat_rows, kv, queries, q_rows,
    acc, totals, attended,
    load_sem, mod_send, mod_recv, gate_send, gate_recv, row_send, row_recv,
    kv_send, kv_recv, q_send, q_recv, w_send, w_recv, att_send, att_recv,
):
    me = lax.axis_index("seq")
    part = lax.axis_index("tensor")
    pair = 2
    side = lax.rem(me, pair)
    mate = me + pair * (1 - 2 * lax.rem(me // pair, 2))
    rows, width = lat.shape
    columns = updated_ref.shape[1]
    head_size = q_gain_ref.shape[1]
    heads = queries.shape[1] // head_size

    def remote(src, dst, send, recv, axis, target):
        return pltpu.make_async_remote_copy(
            src_ref=src, dst_ref=dst, send_sem=send, recv_sem=recv,
            device_id={axis: target}, device_id_type=pl.DeviceIdType.MESH,
        )

    loads = [
        pltpu.make_async_copy(ada_hbm, ada, load_sem.at[0]),
        pltpu.make_async_copy(lat_hbm, lat, load_sem.at[1]),
        pltpu.make_async_copy(qkv_hbm.at[1], wqkv.at[1], load_sem.at[2]),
        pltpu.make_async_copy(qkv_hbm.at[2], wqkv.at[2], load_sem.at[3]),
        pltpu.make_async_copy(qkv_hbm.at[0], wqkv.at[0], load_sem.at[4]),
        pltpu.make_async_copy(
            out_hbm.at[:, pl.ds(pl.multiple_of(part * columns, 128), columns)],
            wout.at[part], load_sem.at[5],
        ),
        pltpu.make_async_copy(noise_hbm, noise, load_sem.at[6]),
    ]
    small = [
        pltpu.make_async_copy(source, held, load_sem.at[7 + index])
        for index, (source, held) in enumerate((
            (level_hbm, level_ref), (head_hbm, head_ref),
            (q_gain_hbm, q_gain_ref), (k_gain_hbm, k_gain_ref),
        ))
    ]
    for load in small:
        load.start()
    for load in loads:
        load.start()

    barrier = pltpu.get_barrier_semaphore()
    for step in range(1, parts):
        pl.semaphore_signal(
            barrier, inc=1, device_id={"tensor": lax.rem(part + step, parts)},
            device_id_type=pl.DeviceIdType.MESH,
        )

    @pl.loop(1, n)
    def _(step):
        pl.semaphore_signal(
            barrier, inc=1, device_id={"seq": lax.rem(me + step, n)},
            device_id_type=pl.DeviceIdType.MESH,
        )

    for load in small:
        load.wait()
    half_width = ada.shape[1] // 2
    order = lax.broadcasted_iota(jnp.int32, (16, half_width), 1).astype(F32)
    angles = level_ref[0].astype(F32) * jnp.exp(-math.log(10000.0) * order / half_width)
    waves = jnp.concatenate([jnp.cos(angles), jnp.sin(angles)], axis=1)
    emb = (waves * (1.0 / (1.0 + jnp.exp(-waves)))).astype(BF16)
    loads[0].wait()
    for j in range(2):
        mods[part, j : j + 1, :] = dot(emb, ada[j])[0:1]
    gates[me] = dot(emb, ada[2])[0:1]

    pl.semaphore_wait(barrier, n - 1 + parts - 1)

    def mod_copy(slot, target):
        return remote(
            mods.at[slot], mods.at[slot], mod_send.at[target], mod_recv.at[slot], "tensor", target
        )

    for step in range(1, parts):
        mod_copy(part, lax.rem(part + step, parts)).start()


    def slab_of(device):
        return pl.multiple_of((device * clean_rows) // slab * slab, slab)

    first_column = pl.multiple_of(part * columns, 128)

    def gate_copy(slot, target):
        return remote(
            gates.at[slot], gates.at[slot], gate_send.at[target], gate_recv.at[slot], "seq", target
        )

    def row_copy(slot, target):
        return remote(
            lat_hbm.at[pl.ds(slab_of(target), slab), pl.ds(first_column, columns)],
            lat_rows.at[slot], row_send.at[target], row_recv.at[slot], "seq", target,
        )

    def w_copy(slot, target):
        at = pl.ds(pl.multiple_of(target * columns, 128), columns)
        return remote(
            out_hbm.at[:, at], wout.at[slot], w_send.at[target], w_recv.at[slot], "tensor", target
        )

    @pl.loop(1, n)
    def _(step):
        target = lax.rem(me + step, n)
        gate_copy(me, target).start()
        row_copy(me, target).start()

    for step in range(1, parts):
        w_copy(part, lax.rem(part + step, parts)).start()

    loads[1].wait()
    own_slab = slab_of(me)
    lat_rows[me] = lat[pl.ds(own_slab, slab), pl.ds(first_column, columns)]

    tile = 16

    @pl.loop(0, rows // tile)
    def _(index):
        at = pl.ds(pl.multiple_of(index * tile, tile), tile)
        states = lat[at, :].astype(F32)
        centered = states - jnp.mean(states, axis=-1, keepdims=True)
        variance = jnp.mean(centered * centered, axis=-1, keepdims=True)
        normed[at, :] = centered * lax.rsqrt(variance + EPS)

    for step in range(1, parts):
        mod_copy(lax.rem(part + step, parts), part).wait_recv()
    for index in range(parts):
        at = slice(index * columns, (index + 1) * columns)
        hidden[:, at] = (
            normed[:, at] * (1.0 + mods[index, 1:2, :]) + mods[index, 0:1, :]
        ).astype(BF16)

    def scaled(matrix, gain, factor):
        power = jnp.mean(matrix * matrix, axis=-1, keepdims=True)
        return (matrix * lax.rsqrt(power + EPS) * gain * factor).astype(BF16)

    def kv_copy(kind, slot, way, target):
        return remote(
            kv.at[slot, kind], kv.at[slot, kind],
            kv_send.at[kind, way, slot], kv_recv.at[kind, slot], "seq", target,
        )

    def onward(kind, slot, way, act):
        target = (me - pair, me + pair, me + 1 - 2 * side)[way]
        there = (target >= 0, target < n, None)[way]
        run = functools.partial(act, kind, slot, way, target)
        if there is None:
            run()
        else:
            pl.when(there)(run)

    def hand_across(kind, slot, act):
        if kind == 0:
            onward(kind, slot, 2, act)
        else:
            pl.when(slot != mate)(lambda: onward(kind, slot, 2, act))

    def start(kind, slot, way, target):
        kv_copy(kind, slot, way, target).start()

    def finish(kind, slot, way, target):
        kv_copy(kind, slot, way, target).wait_send()

    def spread_out(kind, slot):
        for way in range(3):
            onward(kind, slot, way, start)

    def q_copy(slot, target):
        return remote(
            queries.at[pl.ds(slab_of(target), slab), :], q_rows.at[slot],
            q_send.at[target], q_recv.at[slot], "seq", target,
        )

    def head_at(index):
        return slice(index * head_size, (index + 1) * head_size)

    loads[2].wait()
    raw = dot(hidden[...], wqkv[1])
    for h in range(heads):
        kv[me, 0, :, head_at(h)] = scaled(raw[:, head_at(h)], k_gain_ref[...], 1.0)

    spread_out(0, me)

    loads[3].wait()
    kv[me, 1] = dot(hidden[...], wqkv[2]).astype(BF16)

    spread_out(1, me)

    loads[4].wait()
    raw = dot(hidden[...], wqkv[0])
    for h in range(heads):
        queries[:, head_at(h)] = scaled(
            raw[:, head_at(h)], q_gain_ref[...], 1.0 / math.sqrt(head_size)
        )
    q_rows[me] = queries[pl.ds(own_slab, slab), :]

    @pl.loop(1, n)
    def _(step):
        target = lax.rem(me + step, n)
        q_copy(me, target).start()

    oldest = head_ref[0]
    own_rank = lax.rem(me - oldest + n, n)

    for h in range(heads):
        weights = jnp.exp(dot_t(queries[:, head_at(h)], kv[me, 0, :, head_at(h)]))
        totals[:, head_at(h)] = weights
        acc[:, head_at(h)] = dot(weights.astype(BF16), kv[me, 1, :, head_at(h)])

    def absorb(source):
        rank = lax.rem(source - oldest + n, n)
        seen = jnp.full((rows, rows), rank, jnp.int32) <= own_rank
        for h in range(heads):
            scores = dot_t(queries[:, head_at(h)], kv[source, 0, :, head_at(h)])
            weights = jnp.where(seen, jnp.exp(scores), 0.0)
            totals[:, head_at(h)] += weights
            acc[:, head_at(h)] += dot(weights.astype(BF16), kv[source, 1, :, head_at(h)])

    def take_across(source):
        kv_copy(0, source, 2, me).wait_recv()
        kv_copy(1, source, 2, me).wait_recv()
        absorb(source)

    other = me + 1 - 2 * side
    mate_other = mate + 1 - 2 * side

    @pl.loop(1, n // pair)
    def _(step):
        below, above = me - step * pair, me + step * pair
        for kind in range(2):

            @pl.when(below >= 0)
            def _():
                kv_copy(kind, below, 1, me).wait_recv()
                onward(kind, below, 1, start)
                hand_across(kind, below, start)

            @pl.when(above < n)
            def _():
                kv_copy(kind, above, 0, me).wait_recv()
                onward(kind, above, 0, start)
                hand_across(kind, above, start)

        @pl.when(step == 1)
        def _():
            take_across(other)

        @pl.when(step == min(2, n // pair - 1))
        def _():
            kv_copy(1, other, 0, mate).start()

        before, after = other - (step - 1) * pair, other + (step - 1) * pair

        @pl.when((step > 1) & (before >= 0) & (before != mate_other))
        def _():
            take_across(before)

        @pl.when((step > 1) & (after < n) & (after != mate_other))
        def _():
            take_across(after)

        @pl.when(below >= 0)
        def _():
            absorb(below)

        @pl.when(above < n)
        def _():
            absorb(above)

    last = n - pair

    @pl.when((other - last >= 0) & (other - last != mate_other))
    def _():
        take_across(other - last)

    @pl.when((other + last < n) & (other + last != mate_other))
    def _():
        take_across(other + last)

    take_across(mate_other)

    @pl.loop(1, n)
    def _(step):
        source = lax.rem(me - step + n, n)
        q_copy(source, me).wait_recv()
        gate_copy(source, me).wait_recv()
        row_copy(source, me).wait_recv()

    for h in range(heads):
        total = jnp.sum(totals[:, head_at(h)], axis=-1, keepdims=True)
        attended[part, 0:rows, head_at(h)] = (acc[:, head_at(h)] / total).astype(BF16)
        weights = jnp.exp(dot_t(q_rows[oldest, :, head_at(h)], kv[oldest, 0, :, head_at(h)]))
        total = jnp.sum(weights, axis=-1, keepdims=True)
        product = dot(weights.astype(BF16), kv[oldest, 1, :, head_at(h)])
        attended[part, rows:, head_at(h)] = (product / total).astype(BF16)

    core = lax.rem(part, 2)
    sibling = part + 1 - 2 * core

    def att_copy(slot, target, way):
        return remote(
            attended.at[slot], attended.at[slot], att_send.at[way], att_recv.at[slot],
            "tensor", target,
        )

    ahead = [lax.rem(part + 2 * step, parts) for step in range(1, parts // 2)]
    for way, target in enumerate(ahead):
        att_copy(part, target, way).start()
    att_copy(part, sibling, len(ahead)).start()

    loads[5].wait()
    total = dot(attended[part], wout[part])

    def add(slot, total):
        w_copy(slot, part).wait_recv()
        return total + dot(attended[slot], wout[slot])

    att_copy(sibling, part, 0).wait_recv()
    total = add(sibling, total)
    for way, slot in enumerate(ahead):
        att_copy(slot, part, 0).wait_recv()
        att_copy(slot, sibling, len(ahead) + 1 + way).start()
        total = add(slot, total)
    for slot in ahead:
        handed = slot + 1 - 2 * core
        att_copy(handed, part, 0).wait_recv()
        total = add(handed, total)

    own_states = lat[:, pl.ds(first_column, columns)].astype(F32)
    updated = (own_states + gates[me] * total[0:rows]).astype(BF16)
    leaving = jnp.full((rows, columns), own_rank, jnp.int32) == 0
    loads[6].wait()
    updated_ref[0:rows, :] = jnp.where(leaving, noise[...], updated)
    updated_ref[rows:, :] = (
        lat_rows[oldest].astype(F32) + gates[oldest] * total[rows:]
    ).astype(BF16)

    for way in range(parts - 1):
        att_copy(part, sibling, way).wait_send()
    for step in range(1, parts):
        target = lax.rem(part + step, parts)
        mod_copy(part, target).wait_send()
        w_copy(part, target).wait_send()

    @pl.loop(1, n)
    def _(step):
        target = lax.rem(me + step, n)
        q_copy(me, target).wait_send()
        gate_copy(me, target).wait_send()
        row_copy(me, target).wait_send()

    kv_copy(1, other, 0, mate).wait_send()
    for kind in range(2):
        for way in range(3):
            onward(kind, me, way, finish)

    @pl.loop(1, n // pair)
    def _(step):
        below, above = me - step * pair, me + step * pair
        for kind in range(2):

            @pl.when(below >= 0)
            def _():
                onward(kind, below, 1, finish)
                hand_across(kind, below, finish)

            @pl.when(above < n)
            def _():
                onward(kind, above, 0, finish)
                hand_across(kind, above, finish)


def finish_kernel(updated_ref, window_ref, clean_ref):
    rows = window_ref.shape[0]
    window_ref[...] = updated_ref[0:rows, :]
    clean_ref[...] = updated_ref[rows:, :]


def local(
    latents, levels, head_slot, fresh_noise, ada_weight, qkv_weight, q_gain, k_gain, out_weight
):
    n = lax.axis_size("seq")
    parts = lax.axis_size("tensor")
    rows, width = latents.shape
    columns = fresh_noise.shape[1]
    inner = out_weight.shape[0]
    clean_rows = rows // n
    slab = max(clean_rows, 16)
    vmem = pl.BlockSpec(memory_space=pltpu.VMEM)
    hbm = pl.BlockSpec(memory_space=pltpu.HBM)
    dma = pltpu.SemaphoreType.DMA
    updated = pl.pallas_call(
        functools.partial(kernel, n, parts, slab, clean_rows),
        out_shape=jax.ShapeDtypeStruct((rows + slab, columns), BF16),
        in_specs=[
            hbm, hbm, hbm, hbm, hbm, hbm, hbm, hbm, hbm,
        ],
        out_specs=vmem,
        scratch_shapes=[
            pltpu.SMEM((1,), jnp.int32),
            pltpu.SMEM((1,), jnp.int32),
            pltpu.VMEM((1, q_gain.shape[0]), F32),
            pltpu.VMEM((1, q_gain.shape[0]), F32),
            pltpu.VMEM((rows, columns), BF16),
            pltpu.VMEM((rows, width), BF16),
            pltpu.VMEM((3, ada_weight.shape[0], columns), BF16),
            pltpu.VMEM((3, width, inner), BF16),
            pltpu.VMEM((parts, inner, columns), BF16),
            pltpu.VMEM((rows, width), F32),
            pltpu.VMEM((rows, width), BF16),
            pltpu.VMEM((parts, 8, columns), F32),
            pltpu.VMEM((n, 1, columns), F32),
            pltpu.VMEM((n, slab, columns), BF16),
            pltpu.VMEM((n, 2, rows, inner), BF16),
            pltpu.VMEM((rows, inner), BF16),
            pltpu.VMEM((n, slab, inner), BF16),
            pltpu.VMEM((rows, inner), F32),
            pltpu.VMEM((rows, inner), F32),
            pltpu.VMEM((parts, rows + slab, inner), BF16),
            dma((11,)), dma((parts,)), dma((parts,)), dma((n,)), dma((n,)), dma((n,)), dma((n,)),
            dma((2, 3, n)), dma((2, n)), dma((n,)), dma((n,)), dma((parts,)), dma((parts,)),
            dma((parts,)), dma((parts,)),
        ],
        compiler_params=pltpu.CompilerParams(
            collective_id=0, has_side_effects=True, vmem_limit_bytes=60 * 1024 * 1024
        ),
    )(
        head_slot, levels, q_gain.reshape(1, -1), k_gain.reshape(1, -1), fresh_noise, latents,
        jnp.transpose(ada_weight, (1, 0, 2)), jnp.transpose(qkv_weight, (1, 0, 2)), out_weight,
    )
    window, clean = pl.pallas_call(
        finish_kernel,
        out_shape=(
            jax.ShapeDtypeStruct((rows, columns), BF16),
            jax.ShapeDtypeStruct((slab, columns), BF16),
        ),
        in_specs=[vmem],
        out_specs=(vmem, vmem),
    )(updated)
    if clean_rows < slab:
        start = (lax.axis_index("seq") * clean_rows) % slab
        clean = lax.dynamic_slice_in_dim(clean, start, clean_rows, 0)
    return window, clean


def solution(mesh):
    return jax.shard_map(
        local,
        mesh=mesh,
        in_specs=(
            P("seq", None),
            P("seq"),
            P(),
            P(None, "tensor"),
            P(None, None, "tensor"),
            P(None, None, "tensor"),
            P(),
            P(),
            P("tensor", None),
        ),
        out_specs=(P("seq", "tensor"), P("seq", "tensor")),
        check_vma=False,
    )
```
